128 devices in a mesh: ctx: 32 (over z, y, core), head: 2 (over x_lo), section: 2 (over x_hi).
Axes of the slice: x: 4 (x_hi: 2, x_lo: 2; x = x_hi * 2 + x_lo), y: 4, z: 4, core: 2. Of those that a mesh axis runs over, the one named last changes fastest.
Arguments:
- delta_query: bfloat16 [2, 4096, 2048], P('section', 'ctx', 'head'), may hold values from -6 to 6
- delta_key: bfloat16 [2, 4096, 2048], P('section', 'ctx', 'head'), may hold values from -6 to 6
- delta_value: bfloat16 [2, 4096, 2048], P('section', 'ctx', 'head'), may hold values from -6 to 6
- beta_logit: float32 [2, 4096, 16], P('section', 'ctx', 'head'), may hold values from -6 to 6
- decay_input: float32 [2, 4096, 16], P('section', 'ctx', 'head'), may hold values from -4 to 36864
- decay_log: float32 [16], P('head'), may hold values from -14 to -2
- norm_gain: float32 [128], replicated, may hold values from 0.25 to 1.75
- output_gate: bfloat16 [2, 4096, 2048], P('section', 'ctx', 'head'), may hold values from -6 to 6
- delta_cotangent: bfloat16 [2, 4096, 2048], P('section', 'ctx', 'head'), may hold values from -12 to 12
- attn_query: bfloat16 [2, 4096, 4096], P('section', 'ctx', 'head'), may hold values from -5 to 5
- attn_key: bfloat16 [2, 4096, 512], P('section', 'ctx', 'head'), may hold values from -5 to 5
- attn_value: bfloat16 [2, 4096, 512], P('section', 'ctx', 'head'), may hold values from -6 to 6
- attn_gate: bfloat16 [2, 4096, 4096], P('section', 'ctx', 'head'), may hold values from -6 to 6
- attn_cotangent: bfloat16 [2, 4096, 4096], P('section', 'ctx', 'head'), may hold values from -6 to 6
Outputs:
- delta_output: bfloat16 [2, 4096, 2048], P('section', 'ctx', 'head')
- grad_delta_query: bfloat16 [2, 4096, 2048], P('section', 'ctx', 'head')
- grad_delta_key: bfloat16 [2, 4096, 2048], P('section', 'ctx', 'head')
- grad_delta_value: bfloat16 [2, 4096, 2048], P('section', 'ctx', 'head')
- grad_beta_logit: float32 [2, 4096, 16], P('section', 'ctx', 'head')
- grad_decay_input: float32 [2, 4096, 16], P('section', 'ctx', 'head')
- grad_decay_log: float32 [16], P('head')
- grad_norm_gain: float32 [128], replicated
- grad_output_gate: bfloat16 [2, 4096, 2048], P('section', 'ctx', 'head')
- attn_output: bfloat16 [2, 4096, 4096], P('section', 'ctx', 'head')
- grad_attn_query: bfloat16 [2, 4096, 4096], P('section', 'ctx', 'head')
- grad_attn_key: bfloat16 [2, 4096, 512], P('section', 'ctx', 'head')
- grad_attn_value: bfloat16 [2, 4096, 512], P('section', 'ctx', 'head')
- grad_attn_gate: bfloat16 [2, 4096, 4096], P('section', 'ctx', 'head')
The draws below stay inside these ranges and needn't reach their ends.
All inputs are finite; a program needn't handle non-finite values.
Results may differ from the reference program's by a relative error of at most 0.02.
Values may be sent and summed in bfloat16 or wider, within the bound.
A program may use at most 256 MiB of HBM per device.

```python
import math
import jax
import jax.numpy as jnp
from jax import lax

DK = 128
DHEADS = 16
BLOCK_LEN = 64
AHEADS = 16
KVHEADS = 2
AD = 256
TOK_DEV = 128
LENGTH = 4096
SEQS = 2


def decay_pair(key):
    rate_key = jax.random.fold_in(key, 11)
    logs = jax.random.uniform(rate_key, (DHEADS,), jnp.float32, math.log(0.08 / LENGTH), math.log(0.06))
    stochastic_perturbation = 0.7 * jnp.clip(jax.random.normal(jax.random.fold_in(key, 12), (SEQS, LENGTH, DHEADS), jnp.float32), -4.0, 4.0)
    speed_amounts = jnp.exp(logs)
    beginning_shifts = jax.random.uniform(jax.random.fold_in(key, 13), (SEQS, LENGTH // TOK_DEV, DHEADS), jnp.float32, -1.0, 1.0)
    beginning_shifts = jnp.repeat(beginning_shifts, TOK_DEV, axis=1)
    spots = jax.random.randint(jax.random.fold_in(key, 14), (SEQS, 4), 0, LENGTH, dtype=jnp.int32)
    location_sequence = jnp.arange(LENGTH, dtype=jnp.int32)[None, :, None] == spots[:, None, :]
    token_clusters = jnp.any(location_sequence, axis=-1)
    portion_fractions = jax.random.uniform(jax.random.fold_in(key, 15), (SEQS, LENGTH, DHEADS), jnp.float32, 0.25, 0.65)
    opening_multipliers = jnp.where(token_clusters[:, :, None], portion_fractions / speed_amounts[None, None, :], stochastic_perturbation + beginning_shifts)
    return (logs, opening_multipliers)


def draw_decay_log(key, part):
    return decay_pair(key)[0].astype(jnp.float32)


def draw_decay_input(key, part):
    return decay_pair(key)[1].astype(jnp.float32)


def draw_delta_cotangent(key, part):
    positions = jnp.arange(LENGTH, dtype=jnp.float32)[None, :, None] / LENGTH
    drawn = jnp.clip(jax.random.normal(key, (SEQS, LENGTH, DHEADS * DK), jnp.float32), -5.0, 5.0) * (0.5 + 1.5 * positions)
    return drawn.astype(jnp.bfloat16)


def drawn_pair(key):
    query_key = jax.random.fold_in(key, 21)
    keys_key = jax.random.fold_in(key, 22)
    queries = jnp.clip(jax.random.normal(query_key, (SEQS, LENGTH, AHEADS * AD), jnp.float32), -4.5, 4.5)
    keys_drawn = jnp.clip(jax.random.normal(keys_key, (SEQS, LENGTH, KVHEADS * AD), jnp.float32), -4.5, 4.5)
    return (queries, keys_drawn)


def draw_attn_query(key, part):
    return drawn_pair(key)[0].astype(jnp.bfloat16)


def draw_attn_key(key, part):
    return drawn_pair(key)[1].astype(jnp.bfloat16)


def level_of(own_key, extent, split, smallest, largest):
    def one(dim, parts):
        steps = jax.random.uniform(jax.random.fold_in(jax.random.fold_in(own_key, 6), dim), (parts,), jnp.float32, smallest / len(split), largest / len(split))
        return jnp.repeat(jnp.exp(steps), extent[dim] // parts).reshape((-1,) + (1,) * (len(extent) - dim - 1))

    factor_of = one(*split[0])
    for cut in split[1:]:
        factor_of = factor_of * one(*cut)
    return factor_of


def gaussian(key, dims, scale, most, split=(), kind=jnp.bfloat16):
    values = jax.random.normal(key, dims, jnp.float32) * scale
    if len(split) > 0:
        values = level_of(key, dims, split, -0.22, 0.18) * values
    return jnp.clip(values, min=-most, max=most).astype(kind)


def setup_inputs(seed: int = 0) -> dict:
    streams_of = jax.random.split(jax.random.key(seed), 15)
    return {
        "delta_query": gaussian(streams_of[0], (SEQS, LENGTH, DHEADS * DK), 1.0, 6.0, ((0, 2), (1, 32), (2, 2))),
        "delta_key": gaussian(streams_of[1], (SEQS, LENGTH, DHEADS * DK), 1.0, 6.0, ((0, 2), (1, 32), (2, 2))),
        "delta_value": gaussian(streams_of[2], (SEQS, LENGTH, DHEADS * DK), 1.0, 6.0, ((0, 2), (1, 32), (2, 2))),
        "beta_logit": gaussian(streams_of[3], (SEQS, LENGTH, DHEADS), 1.5, 6.0, ((0, 2), (1, 32), (2, 2)), jnp.float32),
        "decay_input": draw_decay_input(jax.random.fold_in(streams_of[14], 71), 0),
        "decay_log": draw_decay_log(jax.random.fold_in(streams_of[14], 71), 0),
        "norm_gain": jnp.clip(1.0 + 0.15 * jax.random.normal(streams_of[6], (DK,), jnp.float32), 0.25, 1.75),
        "output_gate": gaussian(streams_of[7], (SEQS, LENGTH, DHEADS * DK), 1.0, 6.0, ((0, 2), (1, 32), (2, 2))),
        "delta_cotangent": draw_delta_cotangent(jax.random.fold_in(streams_of[14], 71), 0),
        "attn_query": draw_attn_query(jax.random.fold_in(streams_of[14], 71), 0),
        "attn_key": draw_attn_key(jax.random.fold_in(streams_of[14], 71), 0),
        "attn_value": gaussian(streams_of[11], (SEQS, LENGTH, KVHEADS * AD), 1.0, 6.0, ((0, 2), (1, 32), (2, 2))),
        "attn_gate": gaussian(streams_of[12], (SEQS, LENGTH, AHEADS * AD), 1.5, 6.0, ((0, 2), (1, 32), (2, 2))),
        "attn_cotangent": gaussian(streams_of[13], (SEQS, LENGTH, AHEADS * AD), 1.0, 6.0, ((0, 2), (1, 32), (2, 2))),
    }


HIGHEST = lax.Precision.HIGHEST
NEG_FILL = -1e+30

def unit_rows(values):
    return values * lax.rsqrt(lax.optimization_barrier(jnp.sum(values * values, axis=-1, keepdims=True)) + 1e-06)

def decay_inverse(lower_part):
    block_rows = lower_part.shape[-1]
    identity = jnp.eye(block_rows, dtype=jnp.float32)
    result = identity - lower_part
    powered = lower_part
    for doubling in range(block_rows.bit_length() - 2):
        powered = jnp.einsum('hij,hjk->hik', powered, powered, precision=HIGHEST)
        result = jnp.einsum('hij,hjk->hik', result, identity + powered, precision=HIGHEST)
    return result

def split_rows(array, block_rows):
    shaped = array.reshape((array.shape[0] // block_rows, block_rows) + array.shape[1:])
    return jnp.swapaxes(shaped, 1, 2)

def delta_inputs(queries, keys_in, beta_in, decay_in, decay_rates):
    scaling = queries.shape[-1] ** (-0.5)
    unit_queries = unit_rows(queries) * scaling
    unit_keys = unit_rows(keys_in)
    beta_values = jax.nn.sigmoid(beta_in)
    decays = -jnp.exp(decay_rates)[None, :] * jax.nn.softplus(decay_in)
    return (unit_queries, unit_keys, beta_values, decays)

def block_terms(keys_in, values, beta_values, decays):
    block_rows = decays.shape[1]
    cumulative = jnp.cumsum(decays, axis=1)
    row_ids = lax.broadcasted_iota(jnp.int32, (block_rows, block_rows), 0)
    col_ids = lax.broadcasted_iota(jnp.int32, (block_rows, block_rows), 1)
    strict = row_ids > col_ids
    within = row_ids >= col_ids
    spread = cumulative[:, :, None] - cumulative[:, None, :]
    fading = jnp.exp(jnp.where(within, spread, 0.0))
    products = jnp.einsum('hcd,hed->hce', keys_in, keys_in, precision=HIGHEST)
    lower_part = jnp.where(strict, beta_values[:, :, None] * fading * products, 0.0)
    solved = decay_inverse(lower_part)
    value_part = jnp.einsum('hce,hev->hcv', solved, beta_values[:, :, None] * values, precision=HIGHEST)
    key_part = jnp.einsum('hce,hed->hcd', solved, (beta_values * jnp.exp(cumulative))[:, :, None] * keys_in, precision=HIGHEST)
    tail_decay = jnp.exp(cumulative[:, -1:] - cumulative)
    return (cumulative, fading, within, value_part, key_part, tail_decay)

def block_output(state, terms, queries, keys_in):
    cumulative, fading, within, value_part, key_part, tail_decay = terms
    update = value_part - jnp.einsum('hcd,hvd->hcv', key_part, state, precision=HIGHEST)
    scores = jnp.where(within, jnp.einsum('hcd,hed->hce', queries, keys_in, precision=HIGHEST) * fading, 0.0)
    carried = jnp.exp(cumulative)[:, :, None] * jnp.einsum('hcd,hvd->hcv', queries, state, precision=HIGHEST)
    output = carried + jnp.einsum('hce,hev->hcv', scores, update, precision=HIGHEST)
    weighted = tail_decay[:, :, None] * keys_in
    state_next = jnp.exp(cumulative[:, -1])[:, None, None] * state + jnp.einsum('hcv,hcd->hvd', update, weighted, precision=HIGHEST)
    return (output, state_next)

def delta_layer(state, queries, keys_in, values, beta_in, decay_in, decay_rates, gain_in, gate_values, block_rows):
    unit_queries, unit_keys, beta_values, decays = delta_inputs(queries, keys_in, beta_in, decay_in, decay_rates)
    tokens, heads, head_size = queries.shape

    def advance(carried, pieces):
        block_queries, block_keys, block_values, block_betas, block_decays = pieces
        terms = block_terms(block_keys, block_values, block_betas, block_decays)
        output, carried_next = block_output(carried, terms, block_queries, block_keys)
        return (carried_next, output)
    pieces = (split_rows(unit_queries, block_rows), split_rows(unit_keys, block_rows), split_rows(values, block_rows), split_rows(beta_values, block_rows), split_rows(decays, block_rows))
    state_end, outputs = lax.scan(advance, state, pieces)
    mixture = jnp.swapaxes(outputs, 1, 2).reshape(tokens, heads, head_size)
    normed = mixture * lax.rsqrt(lax.optimization_barrier(jnp.mean(mixture * mixture, axis=-1, keepdims=True)) + 1e-06)
    return (normed * gain_in * jax.nn.silu(gate_values), state_end)

def block_scores(queries, key_block, query_start, key_start):
    scores = jnp.einsum('ikgd,jkd->kgij', queries.astype(jnp.float32), key_block.astype(jnp.float32)) * queries.shape[-1] ** (-0.5)
    rows_at = query_start + lax.broadcasted_iota(jnp.int32, (queries.shape[0], key_block.shape[0]), 0)
    cols_at = key_start + lax.broadcasted_iota(jnp.int32, (queries.shape[0], key_block.shape[0]), 1)
    return jnp.where(cols_at <= rows_at, scores, NEG_FILL)

def key_blocks_of(keys_all, values_all):
    length = keys_all.shape[0]
    block_rows = min(512, length)
    block_count = length // block_rows
    key_blocks = keys_all.reshape((block_count, block_rows) + keys_all.shape[1:])
    value_blocks = values_all.reshape((block_count, block_rows) + values_all.shape[1:])
    starts = jnp.arange(block_count, dtype=jnp.int32) * block_rows
    return (key_blocks, value_blocks, starts)

def attend(queries, keys_all, values_all, query_start):
    key_blocks, value_blocks, starts = key_blocks_of(keys_all, values_all)
    stat_shape = (queries.shape[1], queries.shape[2], queries.shape[0])

    def gather_stats(carried, pieces):
        running_max, running_sum = carried
        key_block, key_start = pieces
        scores = block_scores(queries, key_block, query_start, key_start)
        new_max = jnp.maximum(running_max, lax.optimization_barrier(jnp.max(scores, axis=-1)))
        new_sum = running_sum * jnp.exp(running_max - new_max) + lax.optimization_barrier(jnp.sum(jnp.exp(scores - new_max[..., None]), axis=-1))
        return ((new_max, new_sum), None)
    initial = (jnp.full(stat_shape, NEG_FILL, jnp.float32), jnp.zeros(stat_shape, jnp.float32))
    row_max, row_sum = lax.scan(gather_stats, initial, (key_blocks, starts))[0]
    log_total = row_max + jnp.log(row_sum)

    def weigh(running, pieces):
        key_block, value_block, key_start = pieces
        scores = block_scores(queries, key_block, query_start, key_start)
        weights = jnp.exp(scores - log_total[..., None]).astype(jnp.bfloat16)
        return (running + jnp.einsum('kgij,jkd->ikgd', weights.astype(jnp.float32), value_block.astype(jnp.float32)), None)
    attended = lax.scan(weigh, jnp.zeros(queries.shape, jnp.float32), (key_blocks, value_blocks, starts))[0]
    return (attended, log_total)

def key_block_grads(queries, key_block, value_block, query_start, key_start, log_total, upstream, centering):
    scores = block_scores(queries, key_block, query_start, key_start)
    probs = jnp.exp(scores - log_total[..., None])
    weights = probs.astype(jnp.bfloat16).astype(jnp.float32)
    upstream_wide = upstream.astype(jnp.float32)
    value_grad = jnp.einsum('kgij,ikgd->jkd', weights, upstream_wide)
    weight_grad = jnp.einsum('ikgd,jkd->kgij', upstream_wide, value_block.astype(jnp.float32))
    score_grad = (probs * (weight_grad - centering[..., None])).astype(jnp.bfloat16).astype(jnp.float32)
    scaling = queries.shape[-1] ** (-0.5)
    query_grad = jnp.einsum('kgij,jkd->ikgd', score_grad, key_block.astype(jnp.float32)) * scaling
    key_grad = jnp.einsum('kgij,ikgd->jkd', score_grad, queries.astype(jnp.float32)) * scaling
    return (query_grad, key_grad, value_grad)

def attention_grads(queries, keys_all, values_all, query_start, log_total, upstream, centering):
    key_blocks, value_blocks, starts = key_blocks_of(keys_all, values_all)

    def step_grads(running, pieces):
        key_block, value_block, key_start = pieces
        query_grad, key_grad, value_grad = key_block_grads(queries, key_block, value_block, query_start, key_start, log_total, upstream, centering)
        return (running + query_grad, (key_grad, value_grad))
    query_total, stacked = lax.scan(step_grads, jnp.zeros(queries.shape, jnp.float32), (key_blocks, value_blocks, starts))
    return (query_total, stacked[0].reshape(keys_all.shape), stacked[1].reshape(values_all.shape))

def attention_sequence(queries_in, keys_in, values_in, gates_in, cotangent_in):
    group_size = AHEADS // KVHEADS
    block_count = LENGTH // TOK_DEV
    shape_five = (block_count, TOK_DEV, KVHEADS, group_size, AD)
    keys_all = keys_in.reshape(LENGTH, KVHEADS, AD)
    values_all = values_in.reshape(LENGTH, KVHEADS, AD)

    def per_block(running, pieces):
        block_queries, block_gates, block_cotangent, block_index = pieces
        query_start = block_index * TOK_DEV
        attended, log_total = attend(block_queries, keys_all, values_all, query_start)
        opening = jax.nn.sigmoid(block_gates.astype(jnp.float32))
        cotangent_wide = block_cotangent.astype(jnp.float32)
        output = (attended * opening).astype(jnp.bfloat16)
        upstream = (cotangent_wide * opening).astype(jnp.bfloat16)
        gate_grad = (cotangent_wide * attended * opening * (1.0 - opening)).astype(jnp.bfloat16)
        centering = jnp.transpose(lax.optimization_barrier(jnp.sum(upstream.astype(jnp.float32) * attended, axis=-1)), (1, 2, 0))
        query_grad, key_grad, value_grad = attention_grads(block_queries, keys_all, values_all, query_start, log_total, upstream, centering)
        return ((running[0] + key_grad, running[1] + value_grad), (output, query_grad.astype(jnp.bfloat16), gate_grad))
    initial = (jnp.zeros((LENGTH, KVHEADS, AD), jnp.float32), jnp.zeros((LENGTH, KVHEADS, AD), jnp.float32))
    pieces = (queries_in.reshape(shape_five), gates_in.reshape(shape_five), cotangent_in.reshape(shape_five), jnp.arange(block_count, dtype=jnp.int32))
    sums, outputs = lax.scan(per_block, initial, pieces)
    flat = (LENGTH, AHEADS * AD)
    return (outputs[0].reshape(flat), outputs[1].reshape(flat), sums[0].reshape(LENGTH, KVHEADS * AD).astype(jnp.bfloat16), sums[1].reshape(LENGTH, KVHEADS * AD).astype(jnp.bfloat16), outputs[2].reshape(flat))

def reference(delta_query, delta_key, delta_value, beta_logit, decay_input, decay_log, norm_gain, output_gate, delta_cotangent, attn_query, attn_key, attn_value, attn_gate, attn_cotangent):
    blank_state = jnp.zeros((DHEADS, DK, DK), jnp.float32)

    def by_heads(array):
        return array.astype(jnp.float32).reshape(LENGTH, DHEADS, DK)

    def layer_only(queries, keys_in, values, beta_in, decay_in, decay_rates, gain_in, gate_values):
        return delta_layer(blank_state, queries, keys_in, values, beta_in, decay_in, decay_rates, gain_in, gate_values, BLOCK_LEN)[0]
    flat = (LENGTH, DHEADS * DK)
    delta_rows, query_rows, key_rows, value_rows, beta_rows, decay_rows, gate_rows = ([], [], [], [], [], [], [])
    log_grad = jnp.zeros((DHEADS,), jnp.float32)
    gain_grad = jnp.zeros((DK,), jnp.float32)
    attn_rows, attn_query_rows, attn_key_rows, attn_value_rows, attn_gate_rows = ([], [], [], [], [])
    for sequence in range(SEQS):
        result, pullback = jax.vjp(layer_only, by_heads(delta_query[sequence]), by_heads(delta_key[sequence]), by_heads(delta_value[sequence]), beta_logit[sequence], decay_input[sequence], decay_log, norm_gain, by_heads(output_gate[sequence]))
        gradients = pullback(by_heads(delta_cotangent[sequence]))
        delta_rows.append(result.reshape(flat).astype(jnp.bfloat16))
        query_rows.append(gradients[0].reshape(flat).astype(jnp.bfloat16))
        key_rows.append(gradients[1].reshape(flat).astype(jnp.bfloat16))
        value_rows.append(gradients[2].reshape(flat).astype(jnp.bfloat16))
        beta_rows.append(gradients[3])
        decay_rows.append(gradients[4])
        log_grad = log_grad + gradients[5]
        gain_grad = gain_grad + gradients[6]
        gate_rows.append(gradients[7].reshape(flat).astype(jnp.bfloat16))
        attn_parts = attention_sequence(attn_query[sequence], attn_key[sequence], attn_value[sequence], attn_gate[sequence], attn_cotangent[sequence])
        attn_rows.append(attn_parts[0])
        attn_query_rows.append(attn_parts[1])
        attn_key_rows.append(attn_parts[2])
        attn_value_rows.append(attn_parts[3])
        attn_gate_rows.append(attn_parts[4])
    return (jnp.stack(delta_rows), jnp.stack(query_rows), jnp.stack(key_rows), jnp.stack(value_rows), jnp.stack(beta_rows), jnp.stack(decay_rows), log_grad, gain_grad, jnp.stack(gate_rows), jnp.stack(attn_rows), jnp.stack(attn_query_rows), jnp.stack(attn_key_rows), jnp.stack(attn_value_rows), jnp.stack(attn_gate_rows))
```

```python
import functools

import jax
import jax.numpy as jnp
from jax import lax
from jax.experimental import pallas as pl
from jax.experimental.pallas import tpu as pltpu
from jax.sharding import PartitionSpec as P

f32, bf16 = jnp.float32, jnp.bfloat16
MESH = pl.DeviceIdType.MESH
HIGHEST = lax.Precision.HIGHEST
NEG_FILL = -1e30
N = 32
C = 128
DK = 128
AD = 256
HEADS = 8
GROUP = 8
ROWS = GROUP * C
KB = 512
LENGTH = N * C
NKB = LENGTH // KB
QUARTERS = N // HEADS
SROWS = DK // QUARTERS
VMEM_BIG = 60 * 1024 * 1024

NT = (((1,), (1,)), ((), ()))
NN = (((1,), (0,)), ((), ()))
TN = (((0,), (0,)), ((), ()))


def d1(a, b, dims):
    return lax.dot_general(a.astype(bf16), b.astype(bf16), dims, preferred_element_type=f32)


def split(a):
    hi = a.astype(bf16)
    return hi, (a - hi.astype(f32)).astype(bf16)


def d3(a, b, dims):
    ah, al = split(a)
    bh, bl = split(b)

    def dot(x, y):
        return lax.dot_general(x, y, dims, preferred_element_type=f32)

    return dot(ah, bh) + (dot(ah, bl) + dot(al, bh))


def dfull(a, b, dims):
    return lax.dot_general(a, b, dims, precision=HIGHEST, preferred_element_type=f32)


def iotas(shape=(C, C)):
    return (
        lax.broadcasted_iota(jnp.int32, shape, 0),
        lax.broadcasted_iota(jnp.int32, shape, 1),
    )


def unit(x):
    r = lax.rsqrt(jnp.sum(x * x, axis=-1, keepdims=True) + 1e-6)
    return x * r, r


def gates_of(bl_ref, di_ref, dl_ref):
    beta = 1.0 / (1.0 + jnp.exp(-bl_ref[...]))
    a = di_ref[...]
    rate = -jnp.exp(dl_ref[...])
    soft = jnp.maximum(a, 0.0) + jnp.log1p(jnp.exp(-jnp.abs(a)))
    g = jnp.maximum(rate * soft, -104.0)
    r, c = iotas()
    beta_cols = dfull(jnp.where(r == c, 1.0, 0.0), beta, NT)
    cols = dfull(jnp.where(r >= c, 1.0, 0.0), g, NT)
    rows = dfull(g, jnp.where(r <= c, 1.0, 0.0), NN)
    return beta, g, rate, beta_cols, cols, rows


def fade(cc, cr):
    r, c = iotas()
    return jnp.where(r >= c, jnp.exp(jnp.where(r >= c, cc - cr, 0.0)), 0.0)


def head_cols(ref, h):
    return ref[:, h * DK : (h + 1) * DK].astype(f32)


def chunk_kernel(k_ref, v_ref, bl_ref, di_ref, dl_ref, n_ref, w_ref, u0_ref, m_ref, o_ref):
    _, _, _, beta, cols, rows = gates_of(bl_ref, di_ref, dl_ref)
    r, c = iotas()
    group = 4

    for first in range(0, HEADS, group):
        heads = range(first, first + group)
        ks = [unit(head_cols(k_ref, h))[0] for h in heads]
        low = []
        for h, K in zip(heads, ks):
            F = fade(cols[:, h : h + 1], rows[h : h + 1, :])
            low.append(jnp.where(r > c, beta[:, h : h + 1] * F * d1(K, K, NT), 0.0))
        inv = [
            jnp.where(r == c, 1.0, 0.0) - jnp.where(r // 2 == c // 2, L, 0.0) for L in low
        ]
        k = 2
        while k < C:
            part = (r // (2 * k) == c // (2 * k)) & (r // k != c // k)
            mid = [d1(I, jnp.where(part, L, 0.0), NN) for I, L in zip(inv, low)]
            inv = [I - d1(T, I, NN) for I, T in zip(inv, mid)]
            k *= 2
        for h, K, I in zip(heads, ks, inv):
            b, cc = beta[:, h : h + 1], cols[:, h : h + 1]
            V = head_cols(v_ref, h)
            W = d3(I, (b * jnp.exp(cc)) * K, NN)
            U0 = d3(I, b * V, NN)
            cl = cc[C - 1 : C, :]
            Kt = jnp.exp(cl - cc) * K
            n_ref[h] = I
            w_ref[h] = W
            u0_ref[h] = U0
            m_ref[h] = (-d3(W, Kt, TN)).astype(bf16)
            off = d3(U0, Kt, TN)
            keep = jnp.broadcast_to(jnp.exp(cl), (8, DK))
            for q in range(QUARTERS):
                o_ref[h * QUARTERS + q, 0:SROWS, :] = off[q * SROWS : (q + 1) * SROWS, :]
                o_ref[h * QUARTERS + q, SROWS : SROWS + 8, :] = keep


def greet(me):
    barrier = pltpu.get_barrier_semaphore()

    def hello(p, carry):
        pl.semaphore_signal(
            barrier, inc=1, device_id={"ctx": lax.rem(me + p, N)}, device_id_type=MESH
        )
        return carry

    lax.fori_loop(1, N, hello, 0)
    pl.semaphore_wait(barrier, N - 1)


def remote(src, dst, send, recv, peer):
    return pltpu.make_async_remote_copy(
        src_ref=src,
        dst_ref=dst,
        send_sem=send,
        recv_sem=recv,
        device_id={"ctx": peer},
        device_id_type=MESH,
    )


def advanced(S, M, dims):
    hi, lo = split(S)
    both = jnp.concatenate([hi.astype(f32), lo.astype(f32)], axis=0).astype(bf16)
    out = lax.dot_general(both, M, dims, preferred_element_type=f32)
    return out[:SROWS] + out[SROWS:]


def forward_exchange(
    m_ref, o_ref, mall, eall, srecv, oall, sbuf, m_send, m_recv, o_send, o_recv, s_send, s_recv
):
    me = lax.axis_index("ctx")
    greet(me)

    def send(p, carry):
        peer = lax.rem(me + p, N)
        remote(m_ref.at[peer // QUARTERS], mall.at[me], m_send.at[p], m_recv.at[me], peer).start()
        remote(o_ref.at[peer], oall.at[me], o_send.at[p], o_recv.at[me], peer).start()
        return carry

    lax.fori_loop(1, N, send, 0)
    mall[me] = m_ref[me // QUARTERS]
    oall[me] = o_ref[me]

    def step(s, S):
        @pl.when(s != me)
        def _():
            remote(m_ref.at[0], mall.at[s], m_send.at[0], m_recv.at[s], s).wait_recv()
            remote(o_ref.at[0], oall.at[s], o_send.at[0], o_recv.at[s], s).wait_recv()

        sbuf[s] = S

        @pl.when(s != me)
        def _():
            remote(sbuf.at[s], srecv.at[me], s_send.at[s], s_recv.at[me], s).start()

        keep = oall[s, SROWS : SROWS + 8, :]
        eall[s] = keep
        return keep[0:1, :] * S + advanced(S, mall[s], NN) + oall[s, 0:SROWS, :]

    lax.fori_loop(0, N, step, jnp.zeros((SROWS, DK), f32))
    srecv[me] = sbuf[me]

    def finish(p, carry):
        peer = lax.rem(me + p, N)
        remote(m_ref.at[0], mall.at[me], m_send.at[p], m_recv.at[me], peer).wait_send()
        remote(o_ref.at[0], oall.at[me], o_send.at[p], o_recv.at[me], peer).wait_send()
        remote(sbuf.at[peer], srecv.at[me], s_send.at[peer], s_recv.at[me], peer).wait_send()
        remote(sbuf.at[peer], srecv.at[peer], s_send.at[peer], s_recv.at[peer], peer).wait_recv()
        return carry

    lax.fori_loop(1, N, finish, 0)


def backward_exchange(
    mall, eall, l_ref, srecv, lall, sbuf, l_send, l_recv, s_send, s_recv
):
    me = lax.axis_index("ctx")
    greet(me)

    def send(p, carry):
        peer = lax.rem(me + p, N)
        remote(l_ref.at[peer], lall.at[me], l_send.at[p], l_recv.at[me], peer).start()
        return carry

    lax.fori_loop(1, N, send, 0)
    lall[me] = l_ref[me]

    def step(k, S):
        s = N - 1 - k
        sbuf[s] = S

        @pl.when(s != me)
        def _():
            remote(sbuf.at[s], srecv.at[me], s_send.at[s], s_recv.at[me], s).start()
            remote(l_ref.at[0], lall.at[s], l_send.at[0], l_recv.at[s], s).wait_recv()

        return eall[s, 0:1, :] * S + advanced(S, mall[s], NT) + lall[s]

    lax.fori_loop(0, N, step, jnp.zeros((SROWS, DK), f32))
    srecv[me] = sbuf[me]

    def finish(p, carry):
        peer = lax.rem(me + p, N)
        remote(l_ref.at[0], lall.at[me], l_send.at[p], l_recv.at[me], peer).wait_send()
        remote(sbuf.at[peer], srecv.at[me], s_send.at[peer], s_recv.at[me], peer).wait_send()
        remote(sbuf.at[peer], srecv.at[peer], s_send.at[peer], s_recv.at[peer], peer).wait_recv()
        return carry

    lax.fori_loop(1, N, finish, 0)


def output_kernel(
    s_ref, q_ref, k_ref, w_ref, u0_ref, bl_ref, di_ref, dl_ref, gain_ref, gate_ref, cot_ref,
    out_ref, dgate_ref, dgain_ref, u_ref, do_ref, dul_ref, dsl_ref,
):
    _, _, _, _, cols, rows = gates_of(bl_ref, di_ref, dl_ref)
    gain = gain_ref[...]
    gain_sum = jnp.zeros((1, DK), f32)
    for h in range(HEADS):
        at = slice(h * DK, (h + 1) * DK)
        Q = unit(head_cols(q_ref, h))[0] * DK**-0.5
        K = unit(head_cols(k_ref, h))[0]
        S, W = s_ref[h], w_ref[h]
        cc = cols[:, h : h + 1]
        ec = jnp.exp(cc)
        F = fade(cc, rows[h : h + 1, :])
        U = u0_ref[h] - d3(W, S, NT)
        Pm = d3(Q, K, NT) * F
        m = ec * d3(Q, S, NT) + d3(Pm, U, NN)
        rr = lax.rsqrt(jnp.mean(m * m, axis=-1, keepdims=True) + 1e-6)
        gate = head_cols(gate_ref, h)
        cot = head_cols(cot_ref, h)
        sig = 1.0 / (1.0 + jnp.exp(-gate))
        silu = gate * sig
        nm = m * rr
        out_ref[:, at] = (nm * gain * silu).astype(bf16)
        dgate_ref[:, at] = (cot * nm * gain * (sig * (1.0 + gate * (1.0 - sig)))).astype(bf16)
        gain_sum = gain_sum + jnp.sum(cot * nm * silu, axis=0, keepdims=True)
        dn = cot * gain * silu
        dO = rr * dn - m * (rr * rr * rr) * jnp.mean(m * dn, axis=-1, keepdims=True)
        dUl = d3(Pm, dO, TN)
        u_ref[h] = U
        do_ref[h] = dO
        dul_ref[h] = dUl
        dsl_ref[h] = d3(ec * dO, Q, TN) - d3(dUl, W, TN)
    dgain_ref[...] = gain_sum


def gradient_kernel(
    s_ref, ds_ref, q_ref, k_ref, v_ref, n_ref, u_ref, do_ref, dul_ref, bl_ref, di_ref, dl_ref,
    dgain_ref, dq_ref, dk_ref, dv_ref, dbl_ref, ddi_ref, sums_ref,
):
    beta_rows, g, rate, beta, cols, rows = gates_of(bl_ref, di_ref, dl_ref)
    r, c = iotas()
    lane = lax.broadcasted_iota(jnp.int32, (C, DK), 1)
    sub = lax.broadcasted_iota(jnp.int32, (HEADS, C), 0)
    dbeta = jnp.zeros((C, DK), f32)
    dcol = jnp.zeros((C, DK), f32)
    drow = jnp.zeros((HEADS, C), f32)
    dlast = jnp.zeros((HEADS, C), f32)
    for h in range(HEADS):
        at = slice(h * DK, (h + 1) * DK)
        xq, xk = head_cols(q_ref, h), head_cols(k_ref, h)
        Q0, rq = unit(xq)
        Q = Q0 * DK**-0.5
        K, rk = unit(xk)
        V = head_cols(v_ref, h)
        S, dS, I, U, dO, dUl = s_ref[h], ds_ref[h], n_ref[h], u_ref[h], do_ref[h], dul_ref[h]
        b, cc = beta[:, h : h + 1], cols[:, h : h + 1]
        ec = jnp.exp(cc)
        F = fade(cc, rows[h : h + 1, :])
        cl = cc[C - 1 : C, :]
        tail = jnp.exp(cl - cc)
        A = d1(K, K, NT)
        QK = d3(Q, K, NT)
        dU = dUl + d3(tail * K, dS, NT)
        QS = ec * d3(Q, S, NT)
        Y = d3(K, S, NT)
        dPF = d3(dO, U, NT) * F
        dQ = ec * d3(dO, S, NN) + d3(dPF, K, NN)
        dKt = tail * d3(U, dS, NN)
        tau = jnp.sum(dKt * K, axis=-1, keepdims=True)
        dcl = jnp.sum(tau, axis=0, keepdims=True) + jnp.exp(cl) * jnp.sum(
            jnp.sum(dS * S, axis=-1, keepdims=True), axis=0, keepdims=True
        )
        dR = d3(I, dU, TN)
        dV = b * dR
        dY = (-ec) * dV
        dLF = jnp.where(r > c, -d3(dR, U, NT), 0.0) * F
        G2 = dLF * A
        db = jnp.sum(dR * (V - ec * Y), axis=-1, keepdims=True) + jnp.sum(
            G2, axis=-1, keepdims=True
        )
        dA = b * dLF
        dK = d3(dPF, Q, TN) + dKt + d3(dY, S, NN) + d3(dA, K, NN) + d3(dA, K, TN)
        G = dPF * QK + b * G2
        dcc = jnp.sum(dO * QS + dY * Y, axis=-1, keepdims=True) - tau + jnp.sum(
            G, axis=-1, keepdims=True
        )
        dbeta = jnp.where(lane == h, db, dbeta)
        dcol = jnp.where(lane == h, dcc, dcol)
        drow = jnp.where(sub == h, -jnp.sum(G, axis=0, keepdims=True), drow)
        dlast = jnp.where(sub == h, dcl, dlast)
        dq_ref[:, at] = (
            DK**-0.5 * (rq * dQ - xq * (rq * rq * rq) * jnp.sum(xq * dQ, axis=-1, keepdims=True))
        ).astype(bf16)
        dk_ref[:, at] = (
            rk * dK - xk * (rk * rk * rk) * jnp.sum(xk * dK, axis=-1, keepdims=True)
        ).astype(bf16)
        dv_ref[:, at] = dV.astype(bf16)
    later = jnp.where(r >= c, 1.0, 0.0)
    dg = dfull(dcol, later, TN)[:HEADS] + dfull(drow, later, NN) + dlast
    dbeta = dfull(dbeta, jnp.where(r == c, 1.0, 0.0), TN)[:HEADS]
    dbl_ref[...] = dbeta * beta_rows * (1.0 - beta_rows)
    ddi_ref[...] = dg * rate / (1.0 + jnp.exp(-di_ref[...]))
    per_head = jnp.sum(dg * g, axis=1, keepdims=True)
    sums_ref[0:HEADS, :] = jnp.broadcast_to(per_head, (HEADS, DK))
    sums_ref[HEADS : 2 * HEADS, :] = jnp.broadcast_to(dgain_ref[...], (HEADS, DK))


def sum_kernel(x_ref, out_ref, every, part, others, send1, recv1, send2, recv2):
    me, head, section = (lax.axis_index(a) for a in ("ctx", "head", "section"))
    barrier = pltpu.get_barrier_semaphore()

    def hello(p, carry):
        pl.semaphore_signal(
            barrier, inc=1, device_id={"ctx": lax.rem(me + p, N)}, device_id_type=MESH
        )
        return carry

    lax.fori_loop(1, N, hello, 0)
    turns = ((0, 1), (1, 0), (1, 1))

    def aside(dh, ds):
        return {"head": lax.rem(head + dh, 2), "section": lax.rem(section + ds, 2)}

    for dh, ds in turns:
        pl.semaphore_signal(barrier, inc=1, device_id=aside(dh, ds), device_id_type=MESH)
    pl.semaphore_wait(barrier, N + 2)

    def send(p, carry):
        peer = lax.rem(me + p, N)
        remote(x_ref, every.at[me], send1.at[p], recv1.at[me], peer).start()
        return carry

    lax.fori_loop(1, N, send, 0)
    every[me] = x_ref[...]

    def finish(p, carry):
        peer = lax.rem(me + p, N)
        remote(x_ref, every.at[me], send1.at[p], recv1.at[me], peer).wait_send()
        remote(x_ref, every.at[peer], send1.at[p], recv1.at[peer], peer).wait_recv()
        return carry

    lax.fori_loop(1, N, finish, 0)
    part[...] = jnp.sum(every[...], axis=0)
    copies = [
        pltpu.make_async_remote_copy(
            src_ref=part,
            dst_ref=others.at[i],
            send_sem=send2.at[i],
            recv_sem=recv2.at[i],
            device_id=aside(dh, ds),
            device_id_type=MESH,
        )
        for i, (dh, ds) in enumerate(turns)
    ]
    for copy in copies:
        copy.start()
    for copy in copies:
        copy.wait()
    same = slice(0, HEADS)
    gain = slice(HEADS, 2 * HEADS)
    out_ref[same, :] = part[same, :] + others[0, same, :]
    out_ref[gain, :] = (part[gain, :] + others[0, gain, :]) + (
        others[1, gain, :] + others[2, gain, :]
    )


def attention_kernel(
    q_ref, gate_ref, cot_ref, kv_ref,
    out_ref, dq_ref, dgate_ref, dkv_ref,
    qs, ups, probs, att, dqt, top, low, cent,
):
    me = lax.axis_index("ctx")
    blocks = me // (KB // C) + 1
    scale = AD**-0.5
    width = 256
    parts = ROWS // width
    for g in range(GROUP):
        qs[g * C : (g + 1) * C, :] = (
            q_ref[:, g * AD : (g + 1) * AD].astype(f32) * scale
        ).astype(bf16)
    top[...] = jnp.full((8, ROWS), NEG_FILL, f32)
    low[...] = jnp.zeros((8, ROWS), f32)
    att[...] = jnp.zeros((AD, ROWS), f32)
    dqt[...] = jnp.zeros((AD, ROWS), f32)
    key_at, query_at = iotas((KB, width))
    reach = me * C + lax.rem(query_at, C) - key_at

    def rows_of(kb):
        return pl.ds(pl.multiple_of(kb * KB, KB), KB)

    def score(kb, carry):
        keys = kv_ref[rows_of(kb), 0:AD]
        for i in range(parts):
            cols = slice(i * width, (i + 1) * width)
            s = lax.dot_general(keys, qs[cols, :], NT, preferred_element_type=f32)
            s = jnp.where(reach >= kb * KB, s, NEG_FILL)
            probs[rows_of(kb), cols] = s
            top[:, cols] = jnp.maximum(
                top[:, cols], jnp.max(s.reshape(KB // 8, 8, width), axis=0)
            )
        return carry

    lax.fori_loop(0, blocks, score, 0)
    peak = jnp.max(top[...], axis=0, keepdims=True)
    top[...] = jnp.broadcast_to(peak, (8, ROWS))

    def weigh(kb, carry):
        values = kv_ref[rows_of(kb), AD : 2 * AD]
        for i in range(parts):
            cols = slice(i * width, (i + 1) * width)
            p = jnp.exp(probs[rows_of(kb), cols] - top[0:1, cols])
            probs[rows_of(kb), cols] = p
            low[:, cols] = low[:, cols] + jnp.sum(p.reshape(KB // 8, 8, width), axis=0)
            att[:, cols] = att[:, cols] + lax.dot_general(
                values, p.astype(bf16), TN, preferred_element_type=f32
            )
        return carry

    lax.fori_loop(0, blocks, weigh, 0)
    share = 1.0 / jnp.sum(low[...], axis=0, keepdims=True)
    low[...] = jnp.broadcast_to(share, (8, ROWS))
    for g in range(GROUP):
        cols = slice(g * C, (g + 1) * C)
        at = slice(g * AD, (g + 1) * AD)
        attended = jnp.transpose(att[:, cols] * low[0:1, cols])
        opening = 1.0 / (1.0 + jnp.exp(-gate_ref[:, at].astype(f32)))
        cot = cot_ref[:, at].astype(f32)
        out_ref[:, at] = (attended * opening).astype(bf16)
        up = (cot * opening).astype(bf16)
        ups[cols, :] = up
        dgate_ref[:, at] = (cot * attended * opening * (1.0 - opening)).astype(bf16)
        center = jnp.sum(jnp.transpose(up.astype(f32) * attended), axis=0, keepdims=True)
        cent[:, cols] = jnp.broadcast_to(center, (8, C))

    def grads(kb, carry):
        keys = kv_ref[rows_of(kb), 0:AD]
        values = kv_ref[rows_of(kb), AD : 2 * AD]
        dk = jnp.zeros((KB, AD), f32)
        dv = jnp.zeros((KB, AD), f32)
        for i in range(parts):
            cols = slice(i * width, (i + 1) * width)
            p = probs[rows_of(kb), cols] * low[0:1, cols]
            dp = lax.dot_general(values, ups[cols, :], NT, preferred_element_type=f32)
            ds = (p * (dp - cent[0:1, cols])).astype(bf16)
            dv = dv + lax.dot_general(p.astype(bf16), ups[cols, :], NN, preferred_element_type=f32)
            dk = dk + lax.dot_general(ds, qs[cols, :], NN, preferred_element_type=f32)
            dqt[:, cols] = dqt[:, cols] + lax.dot_general(
                keys, ds, TN, preferred_element_type=f32
            )
        dkv_ref[rows_of(kb), 0:AD] = dk
        dkv_ref[rows_of(kb), AD : 2 * AD] = dv
        return carry

    lax.fori_loop(0, blocks, grads, 0)

    def blank(kb, carry):
        dkv_ref[rows_of(kb), :] = jnp.zeros((KB, 2 * AD), f32)
        return carry

    lax.fori_loop(blocks, NKB, blank, 0)
    for g in range(GROUP):
        cols = slice(g * C, (g + 1) * C)
        dq_ref[:, g * AD : (g + 1) * AD] = (jnp.transpose(dqt[:, cols]) * scale).astype(bf16)


VM = pl.BlockSpec(memory_space=pltpu.VMEM)


def call(kernel, outs, args, scratch=(), collective=None):
    options = {"vmem_limit_bytes": VMEM_BIG}
    if collective is not None:
        options.update(collective_id=collective, has_side_effects=True)
    return pl.pallas_call(
        kernel,
        out_shape=tuple(jax.ShapeDtypeStruct(s, d) for s, d in outs),
        in_specs=[VM] * len(args),
        out_specs=tuple(VM for _ in outs),
        scratch_shapes=list(scratch),
        compiler_params=pltpu.CompilerParams(**options),
    )(*args)


SQ = (HEADS, DK, DK)


def per_device(
    delta_query, delta_key, delta_value, beta_logit, decay_input, decay_log, norm_gain,
    output_gate, delta_cotangent, attn_query, attn_key, attn_value, attn_gate, attn_cotangent,
):
    q, k, v = delta_query[0], delta_key[0], delta_value[0]
    gates = (beta_logit[0].T, decay_input[0].T, decay_log[:, None])
    wide = (C, HEADS * DK)
    dma = pltpu.SemaphoreType.DMA((N,))

    kv = jnp.concatenate([attn_key[0], attn_value[0]], axis=-1)
    kv_all = lax.all_gather(kv, "ctx", axis=0, tiled=True)

    inv, w, u0, m, off = call(
        chunk_kernel,
        [(SQ, f32), (SQ, f32), (SQ, f32), (SQ, bf16), ((N, SROWS + 8, DK), f32)],
        (k, v) + gates,
    )
    m_all, keep_all, state = call(
        forward_exchange,
        [((N, DK, DK), bf16), ((N, 8, DK), f32), ((N, SROWS, DK), f32)],
        (m, off),
        [pltpu.VMEM((N, SROWS + 8, DK), f32), pltpu.VMEM((N, SROWS, DK), f32)] + [dma] * 6,
        collective=1,
    )
    kv_all, state = lax.optimization_barrier((kv_all, state))
    flat = (C, GROUP * AD)
    attn_out, attn_dq, attn_dgate, dkv = call(
        attention_kernel,
        [(flat, bf16), (flat, bf16), (flat, bf16), ((LENGTH, 2 * AD), f32)],
        (attn_query[0], attn_gate[0], attn_cotangent[0], kv_all),
        [
            pltpu.VMEM((ROWS, AD), bf16),
            pltpu.VMEM((ROWS, AD), bf16),
            pltpu.VMEM((LENGTH, ROWS), f32),
            pltpu.VMEM((AD, ROWS), f32),
            pltpu.VMEM((AD, ROWS), f32),
            pltpu.VMEM((8, ROWS), f32),
            pltpu.VMEM((8, ROWS), f32),
            pltpu.VMEM((8, ROWS), f32),
        ],
    )
    dkv, state = lax.optimization_barrier((dkv, state))
    own = lax.psum_scatter(dkv, "ctx", scatter_dimension=0, tiled=True)

    state = state.reshape(SQ)
    out, dgate, dgain, u, do, dul, dsl = call(
        output_kernel,
        [(wide, bf16), (wide, bf16), ((1, DK), f32), (SQ, f32), (SQ, f32), (SQ, f32), (SQ, f32)],
        (state, q, k, w, u0) + gates + (norm_gain[None], output_gate[0], delta_cotangent[0]),
    )
    (dstate,) = call(
        backward_exchange,
        [((N, SROWS, DK), f32)],
        (m_all, keep_all, dsl.reshape(N, SROWS, DK)),
        [pltpu.VMEM((N, SROWS, DK), f32), pltpu.VMEM((N, SROWS, DK), f32)] + [dma] * 4,
        collective=2,
    )
    pair = (2 * HEADS, DK)
    rows = (HEADS, C)
    dq, dk, dv, dbl, ddi, sums = call(
        gradient_kernel,
        [(wide, bf16), (wide, bf16), (wide, bf16), (rows, f32), (rows, f32), (pair, f32)],
        (state, dstate.reshape(SQ), q, k, v, inv, u, do, dul) + gates + (dgain,),
    )
    (sums,) = call(
        sum_kernel,
        [(pair, f32)],
        (sums,),
        [pltpu.VMEM((N,) + pair, f32), pltpu.VMEM(pair, f32), pltpu.VMEM((3,) + pair, f32)]
        + [dma] * 2
        + [pltpu.SemaphoreType.DMA((3,))] * 2,
        collective=3,
    )
    log_grad, gain_grad = sums[:HEADS, 0], sums[HEADS]
    return (
        out[None], dq[None], dk[None], dv[None], dbl.T[None], ddi.T[None], log_grad, gain_grad,
        dgate[None], attn_out[None], attn_dq[None],
        own[:, :AD].astype(bf16)[None], own[:, AD:].astype(bf16)[None], attn_dgate[None],
    )


def solution(mesh):
    split3 = P("section", "ctx", "head")
    in_specs = (split3,) * 5 + (P("head"), P()) + (split3,) * 7
    out_specs = (split3,) * 6 + (P("head"), P()) + (split3,) * 6
    return jax.shard_map(
        per_device, mesh=mesh, in_specs=in_specs, out_specs=out_specs, check_vma=False
    )
```

```python
import functools

import jax
import jax.numpy as jnp
from jax import lax
from jax.experimental import pallas as pl
from jax.experimental.pallas import tpu as pltpu
from jax.sharding import PartitionSpec as P

f32, bf16 = jnp.float32, jnp.bfloat16
MESH = pl.DeviceIdType.MESH
HIGHEST = lax.Precision.HIGHEST
NEG_FILL = -1e30
N = 32
C = 128
DK = 128
AD = 256
HEADS = 8
GROUP = 8
ROWS = GROUP * C
KB = 512
LENGTH = N * C
NKB = LENGTH // KB
QUARTERS = N // HEADS
SROWS = DK // QUARTERS
KEEP = 16
CHIPS = N // 2
VMEM_BIG = 60 * 1024 * 1024

NT = (((1,), (1,)), ((), ()))
NN = (((1,), (0,)), ((), ()))
TN = (((0,), (0,)), ((), ()))


def d1(a, b, dims):
    return lax.dot_general(a.astype(bf16), b.astype(bf16), dims, preferred_element_type=f32)


def split(a):
    hi = a.astype(bf16)
    return hi, (a - hi.astype(f32)).astype(bf16)


def d3(a, b, dims):
    ah, al = split(a)
    bh, bl = split(b)

    def dot(x, y):
        return lax.dot_general(x, y, dims, preferred_element_type=f32)

    return dot(ah, bh) + (dot(ah, bl) + dot(al, bh))


def dfull(a, b, dims):
    return lax.dot_general(a, b, dims, precision=HIGHEST, preferred_element_type=f32)


def iotas(shape=(C, C)):
    return (
        lax.broadcasted_iota(jnp.int32, shape, 0),
        lax.broadcasted_iota(jnp.int32, shape, 1),
    )


def unit(x):
    r = lax.rsqrt(jnp.sum(x * x, axis=-1, keepdims=True) + 1e-6)
    return x * r, r


def gates_of(bl_ref, di_ref, dl_ref):
    beta = 1.0 / (1.0 + jnp.exp(-bl_ref[...]))
    a = di_ref[...]
    head = lax.broadcasted_iota(jnp.int32, a.shape, 0)
    logs = jnp.zeros(a.shape, f32)
    for h in range(HEADS):
        logs = jnp.where(head == h, dl_ref[h], logs)
    rate = -jnp.exp(logs)
    soft = jnp.maximum(a, 0.0) + jnp.log1p(jnp.exp(-jnp.abs(a)))
    g = jnp.maximum(rate * soft, -104.0)
    r, c = iotas()
    beta_cols = dfull(jnp.where(r == c, 1.0, 0.0), beta, NT)
    cols = dfull(jnp.where(r >= c, 1.0, 0.0), g, NT)
    rows = dfull(g, jnp.where(r <= c, 1.0, 0.0), NN)
    return beta, g, rate, beta_cols, cols, rows


def fade(cc, cr):
    r, c = iotas()
    return jnp.where(r >= c, jnp.exp(jnp.where(r >= c, cc - cr, 0.0)), 0.0)


def head_cols(ref, h):
    return ref[:, h * DK : (h + 1) * DK].astype(f32)


def chunk_kernel(k_ref, v_ref, bl_ref, di_ref, dl_ref, n_ref, w_ref, u0_ref, m_ref, o_ref):
    _, _, _, beta, cols, rows = gates_of(bl_ref, di_ref, dl_ref)
    r, c = iotas()
    group = 4

    for first in range(0, HEADS, group):
        heads = range(first, first + group)
        ks = [unit(head_cols(k_ref, h))[0] for h in heads]
        low = []
        for h, K in zip(heads, ks):
            F = fade(cols[:, h : h + 1], rows[h : h + 1, :])
            low.append(jnp.where(r > c, beta[:, h : h + 1] * F * d1(K, K, NT), 0.0))
        inv = [
            jnp.where(r == c, 1.0, 0.0) - jnp.where(r // 2 == c // 2, L, 0.0) for L in low
        ]
        k = 2
        while k < C:
            part = (r // (2 * k) == c // (2 * k)) & (r // k != c // k)
            mid = [d1(I, jnp.where(part, L, 0.0), NN) for I, L in zip(inv, low)]
            inv = [I - d1(T, I, NN) for I, T in zip(inv, mid)]
            k *= 2
        for h, K, I in zip(heads, ks, inv):
            b, cc = beta[:, h : h + 1], cols[:, h : h + 1]
            V = head_cols(v_ref, h)
            W = d3(I, (b * jnp.exp(cc)) * K, NN)
            U0 = d3(I, b * V, NN)
            cl = cc[C - 1 : C, :]
            Kt = jnp.exp(cl - cc) * K
            n_ref[h] = I
            w_ref[h] = W
            u0_ref[h] = U0
            m_ref[h] = (-d3(W, Kt, TN)).astype(bf16)
            off = d3(U0, Kt, TN).astype(bf16)
            keep = jnp.broadcast_to(jnp.exp(cl), (KEEP, DK))
            high = keep.astype(bf16)
            mid = (keep - high.astype(f32)).astype(bf16)
            last = keep - high.astype(f32) - mid.astype(f32)
            row = lax.broadcasted_iota(jnp.int32, (KEEP, DK), 0)
            terms = jnp.where(row == 0, high.astype(f32), jnp.where(row == 1, mid.astype(f32), last))
            for q in range(QUARTERS):
                o_ref[h * QUARTERS + q, 0:SROWS, :] = off[q * SROWS : (q + 1) * SROWS, :]
                o_ref[h * QUARTERS + q, SROWS : SROWS + KEEP, :] = terms.astype(bf16)


def greet(me):
    barrier = pltpu.get_barrier_semaphore()

    def hello(p, carry):
        pl.semaphore_signal(
            barrier, inc=1, device_id={"ctx": lax.rem(me + p, N)}, device_id_type=MESH
        )
        return carry

    lax.fori_loop(1, N, hello, 0)
    pl.semaphore_wait(barrier, N - 1)


def remote(src, dst, send, recv, peer):
    return pltpu.make_async_remote_copy(
        src_ref=src,
        dst_ref=dst,
        send_sem=send,
        recv_sem=recv,
        device_id={"ctx": peer},
        device_id_type=MESH,
    )


def forward_exchange(
    m_ref, o_ref, mall, eall, srecv, oall, sbuf,
    m_send, m_recv, f_send, f_recv, o_send, o_recv, s_send, s_recv,
):
    me = lax.axis_index("ctx")
    core = lax.rem(me, 2)
    chip = me // 2
    mate = chip * 2 + 1 - core
    greet(me)

    def to_core(p):
        return lax.rem(chip + p, CHIPS) * 2 + core

    def send_map(p, carry):
        peer = to_core(p)
        remote(m_ref.at[peer // QUARTERS], mall.at[me], m_send.at[p], m_recv.at[me], peer).start()
        return carry

    def send_offset(p, carry):
        peer = lax.rem(me + p, N)
        remote(o_ref.at[peer], oall.at[me], o_send.at[p], o_recv.at[me], peer).start()
        return carry

    lax.fori_loop(1, CHIPS, send_map, 0)
    lax.fori_loop(1, N, send_offset, 0)
    mall[me] = m_ref[me // QUARTERS]
    oall[me] = o_ref[me]

    def hand_over(source):
        return remote(mall.at[source], mall.at[source], f_send.at[source], f_recv.at[source], mate)

    def arrive(c):
        source = 2 * c + core

        @pl.when(source != me)
        def _():
            remote(m_ref.at[0], mall.at[source], m_send.at[0], m_recv.at[source], source).wait_recv()

        hand_over(source).start()

    def advance(s, S):
        @pl.when(s != me)
        def _():
            remote(o_ref.at[0], oall.at[s], o_send.at[0], o_recv.at[s], s).wait_recv()

        sbuf[s] = S.astype(bf16)

        @pl.when(s != me)
        def _():
            remote(sbuf.at[s], srecv.at[me], s_send.at[s], s_recv.at[me], s).start()

        terms = oall[s, SROWS : SROWS + KEEP, :].astype(f32)
        keep = terms[0:1] + (terms[1:2] + terms[2:3])
        eall[s] = jnp.broadcast_to(keep, (8, DK))
        return keep * S + d1(S, mall[s], NN) + oall[s, 0:SROWS, :].astype(f32)

    def pair(c, S):
        other = 2 * c + 1 - core
        hand_over(other).wait_recv()
        return advance(2 * c + 1, advance(2 * c, S))

    def step(c, S):
        arrive(c)
        return pair(c - 1, S)

    arrive(0)
    S = lax.fori_loop(1, CHIPS, step, jnp.zeros((SROWS, DK), f32))
    pair(CHIPS - 1, S)
    srecv[me] = sbuf[me]

    def finish_map(p, carry):
        peer = to_core(p)
        remote(m_ref.at[0], mall.at[me], m_send.at[p], m_recv.at[me], peer).wait_send()
        return carry

    def finish_pass(c, carry):
        hand_over(2 * c + core).wait_send()
        return carry

    def finish(p, carry):
        peer = lax.rem(me + p, N)
        remote(o_ref.at[0], oall.at[me], o_send.at[p], o_recv.at[me], peer).wait_send()
        remote(sbuf.at[peer], srecv.at[me], s_send.at[peer], s_recv.at[me], peer).wait_send()
        remote(sbuf.at[peer], srecv.at[peer], s_send.at[peer], s_recv.at[peer], peer).wait_recv()
        return carry

    lax.fori_loop(1, CHIPS, finish_map, 0)
    lax.fori_loop(0, CHIPS, finish_pass, 0)
    lax.fori_loop(1, N, finish, 0)


def backward_exchange(mall, eall, l_ref, srecv, lall, sbuf, l_send, l_recv, s_send, s_recv):
    me = lax.axis_index("ctx")
    greet(me)

    def send(p, carry):
        peer = lax.rem(me + p, N)
        remote(l_ref.at[peer], lall.at[me], l_send.at[p], l_recv.at[me], peer).start()
        return carry

    lax.fori_loop(1, N, send, 0)
    lall[me] = l_ref[me]

    def step(k, S):
        s = N - 1 - k
        sbuf[s] = S.astype(bf16)

        @pl.when(s != me)
        def _():
            remote(sbuf.at[s], srecv.at[me], s_send.at[s], s_recv.at[me], s).start()
            remote(l_ref.at[0], lall.at[s], l_send.at[0], l_recv.at[s], s).wait_recv()

        return eall[s, 0:1, :] * S + d1(S, mall[s], NT) + lall[s].astype(f32)

    lax.fori_loop(0, N, step, jnp.zeros((SROWS, DK), f32))
    srecv[me] = sbuf[me]

    def finish(p, carry):
        peer = lax.rem(me + p, N)
        remote(l_ref.at[0], lall.at[me], l_send.at[p], l_recv.at[me], peer).wait_send()
        remote(sbuf.at[peer], srecv.at[me], s_send.at[peer], s_recv.at[me], peer).wait_send()
        remote(sbuf.at[peer], srecv.at[peer], s_send.at[peer], s_recv.at[peer], peer).wait_recv()
        return carry

    lax.fori_loop(1, N, finish, 0)


def output_kernel(
    s_ref, q_ref, k_ref, w_ref, u0_ref, bl_ref, di_ref, dl_ref, gain_ref, gate_ref, cot_ref,
    out_ref, dgate_ref, dgain_ref, u_ref, do_ref, dul_ref, dsl_ref,
):
    _, _, _, _, cols, rows = gates_of(bl_ref, di_ref, dl_ref)
    gain = gain_ref[...]
    gain_sum = jnp.zeros((1, DK), f32)
    for h in range(HEADS):
        at = slice(h * DK, (h + 1) * DK)
        Q = unit(head_cols(q_ref, h))[0] * DK**-0.5
        K = unit(head_cols(k_ref, h))[0]
        S, W = s_ref[h].astype(f32), w_ref[h]
        cc = cols[:, h : h + 1]
        ec = jnp.exp(cc)
        F = fade(cc, rows[h : h + 1, :])
        U = u0_ref[h] - d3(W, S, NT)
        Pm = d3(Q, K, NT) * F
        m = ec * d3(Q, S, NT) + d3(Pm, U, NN)
        rr = lax.rsqrt(jnp.mean(m * m, axis=-1, keepdims=True) + 1e-6)
        gate = head_cols(gate_ref, h)
        cot = head_cols(cot_ref, h)
        sig = 1.0 / (1.0 + jnp.exp(-gate))
        silu = gate * sig
        nm = m * rr
        out_ref[:, at] = (nm * gain * silu).astype(bf16)
        dgate_ref[:, at] = (cot * nm * gain * (sig * (1.0 + gate * (1.0 - sig)))).astype(bf16)
        gain_sum = gain_sum + jnp.sum(cot * nm * silu, axis=0, keepdims=True)
        dn = cot * gain * silu
        dO = rr * dn - m * (rr * rr * rr) * jnp.mean(m * dn, axis=-1, keepdims=True)
        dUl = d3(Pm, dO, TN)
        u_ref[h] = U
        do_ref[h] = dO
        dul_ref[h] = dUl
        dsl_ref[h] = (d3(ec * dO, Q, TN) - d3(dUl, W, TN)).astype(bf16)
    dgain_ref[...] = gain_sum


def gradient_kernel(
    s_ref, ds_ref, q_ref, k_ref, v_ref, n_ref, u_ref, do_ref, dul_ref, bl_ref, di_ref, dl_ref,
    dgain_ref, dq_ref, dk_ref, dv_ref, dbl_ref, ddi_ref, sums_ref,
):
    beta_rows, g, rate, beta, cols, rows = gates_of(bl_ref, di_ref, dl_ref)
    r, c = iotas()
    lane = lax.broadcasted_iota(jnp.int32, (C, DK), 1)
    sub = lax.broadcasted_iota(jnp.int32, (HEADS, C), 0)
    dbeta = jnp.zeros((C, DK), f32)
    dcol = jnp.zeros((C, DK), f32)
    drow = jnp.zeros((HEADS, C), f32)
    dlast = jnp.zeros((HEADS, C), f32)
    for h in range(HEADS):
        at = slice(h * DK, (h + 1) * DK)
        xq, xk = head_cols(q_ref, h), head_cols(k_ref, h)
        Q0, rq = unit(xq)
        Q = Q0 * DK**-0.5
        K, rk = unit(xk)
        V = head_cols(v_ref, h)
        S, dS = s_ref[h].astype(f32), ds_ref[h].astype(f32)
        I, U, dO, dUl = n_ref[h], u_ref[h], do_ref[h], dul_ref[h]
        b, cc = beta[:, h : h + 1], cols[:, h : h + 1]
        ec = jnp.exp(cc)
        F = fade(cc, rows[h : h + 1, :])
        cl = cc[C - 1 : C, :]
        tail = jnp.exp(cl - cc)
        A = d1(K, K, NT)
        QK = d3(Q, K, NT)
        dU = dUl + d3(tail * K, dS, NT)
        QS = ec * d3(Q, S, NT)
        Y = d3(K, S, NT)
        dPF = d3(dO, U, NT) * F
        dQ = ec * d3(dO, S, NN) + d3(dPF, K, NN)
        dKt = tail * d3(U, dS, NN)
        tau = jnp.sum(dKt * K, axis=-1, keepdims=True)
        dcl = jnp.sum(tau, axis=0, keepdims=True) + jnp.exp(cl) * jnp.sum(
            jnp.sum(dS * S, axis=-1, keepdims=True), axis=0, keepdims=True
        )
        dR = d3(I, dU, TN)
        dV = b * dR
        dY = (-ec) * dV
        dLF = jnp.where(r > c, -d3(dR, U, NT), 0.0) * F
        G2 = dLF * A
        db = jnp.sum(dR * (V - ec * Y), axis=-1, keepdims=True) + jnp.sum(
            G2, axis=-1, keepdims=True
        )
        dA = b * dLF
        dK = d3(dPF, Q, TN) + dKt + d3(dY, S, NN) + d3(dA, K, NN) + d3(dA, K, TN)
        G = dPF * QK + b * G2
        dcc = jnp.sum(dO * QS + dY * Y, axis=-1, keepdims=True) - tau + jnp.sum(
            G, axis=-1, keepdims=True
        )
        dbeta = jnp.where(lane == h, db, dbeta)
        dcol = jnp.where(lane == h, dcc, dcol)
        drow = jnp.where(sub == h, -jnp.sum(G, axis=0, keepdims=True), drow)
        dlast = jnp.where(sub == h, dcl, dlast)
        dq_ref[:, at] = (
            DK**-0.5 * (rq * dQ - xq * (rq * rq * rq) * jnp.sum(xq * dQ, axis=-1, keepdims=True))
        ).astype(bf16)
        dk_ref[:, at] = (
            rk * dK - xk * (rk * rk * rk) * jnp.sum(xk * dK, axis=-1, keepdims=True)
        ).astype(bf16)
        dv_ref[:, at] = dV.astype(bf16)
    later = jnp.where(r >= c, 1.0, 0.0)
    dg = dfull(dcol, later, TN)[:HEADS] + dfull(drow, later, NN) + dlast
    dbeta = dfull(dbeta, jnp.where(r == c, 1.0, 0.0), TN)[:HEADS]
    dbl_ref[...] = dbeta * beta_rows * (1.0 - beta_rows)
    ddi_ref[...] = dg * rate / (1.0 + jnp.exp(-di_ref[...]))
    per_head = jnp.sum(dg * g, axis=1, keepdims=True)
    sums_ref[0:HEADS, :] = jnp.broadcast_to(per_head, (HEADS, DK))
    sums_ref[HEADS : 2 * HEADS, :] = jnp.broadcast_to(dgain_ref[...], (HEADS, DK))


def attention_kernel(
    q_ref, gate_ref, cot_ref, kv_ref, x_ref,
    out_ref, dq_ref, dgate_ref, dk_ref, dv_ref, sums_ref,
    qs, ups, probs, att, dqt, top, low, cent,
    block, keep, give, got, both, taken, total, pairs, every, part, others,
    g_send, g_recv, b_send, b_recv, p_send, p_recv, e_send, e_recv, a_send, a_recv,
):
    me, head, section = (lax.axis_index(a) for a in ("ctx", "head", "section"))
    core = lax.rem(me, 2)
    chip = me // 2
    mate = chip * 2 + 1 - core
    barrier = pltpu.get_barrier_semaphore()

    def to_core(p):
        return lax.rem(chip + p, CHIPS) * 2 + core

    def hello(p, carry):
        pl.semaphore_signal(barrier, inc=1, device_id={"ctx": to_core(p)}, device_id_type=MESH)
        return carry

    turns = ((0, 1), (1, 0), (1, 1))

    def aside(i):
        dh, ds = turns[i]
        return {"head": lax.rem(head + dh, 2), "section": lax.rem(section + ds, 2)}

    lax.fori_loop(1, CHIPS, hello, 0)
    pl.semaphore_signal(barrier, inc=1, device_id={"ctx": mate}, device_id_type=MESH)
    for i in range(3):
        pl.semaphore_signal(barrier, inc=1, device_id=aside(i), device_id_type=MESH)

    def pair_copy():
        return remote(x_ref, pairs, p_send, p_recv, mate)

    def every_copy(p, source):
        return remote(part, every.at[source], e_send.at[p], e_recv.at[source], to_core(p))

    def aside_copy(i):
        return pltpu.make_async_remote_copy(
            src_ref=total,
            dst_ref=others.at[i],
            send_sem=a_send.at[i],
            recv_sem=a_recv.at[i],
            device_id=aside(i),
            device_id_type=MESH,
        )

    blocks = me // (KB // C) + 1
    scale = AD**-0.5
    width = 256
    parts = ROWS // width
    for g in range(GROUP):
        qs[g * C : (g + 1) * C, :] = (
            q_ref[:, g * AD : (g + 1) * AD].astype(f32) * scale
        ).astype(bf16)
    top[...] = jnp.full((8, ROWS), NEG_FILL, f32)
    low[...] = jnp.zeros((8, ROWS), f32)
    att[...] = jnp.zeros((AD, ROWS), f32)
    dqt[...] = jnp.zeros((AD, ROWS), f32)
    key_at, query_at = iotas((KB, width))
    reach = me * C + lax.rem(query_at, C) - key_at

    def rows_of(kb):
        return pl.ds(pl.multiple_of(kb * KB, KB), KB)

    def score(kb, carry):
        keys = kv_ref[rows_of(kb), 0:AD]
        for i in range(parts):
            cols = slice(i * width, (i + 1) * width)
            s = lax.dot_general(keys, qs[cols, :], NT, preferred_element_type=f32)
            s = jnp.where(reach >= kb * KB, s, NEG_FILL)
            probs[rows_of(kb), cols] = s
            top[:, cols] = jnp.maximum(
                top[:, cols], jnp.max(s.reshape(KB // 8, 8, width), axis=0)
            )
        return carry

    lax.fori_loop(0, blocks, score, 0)
    peak = jnp.max(top[...], axis=0, keepdims=True)
    top[...] = jnp.broadcast_to(peak, (8, ROWS))

    def weigh(kb, carry):
        values = kv_ref[rows_of(kb), AD : 2 * AD]
        for i in range(parts):
            cols = slice(i * width, (i + 1) * width)
            p = jnp.exp(probs[rows_of(kb), cols] - top[0:1, cols])
            probs[rows_of(kb), cols] = p
            low[:, cols] = low[:, cols] + jnp.sum(p.reshape(KB // 8, 8, width), axis=0)
            att[:, cols] = att[:, cols] + lax.dot_general(
                values, p.astype(bf16), TN, preferred_element_type=f32
            )
        return carry

    pl.semaphore_wait(barrier, CHIPS + 3)
    pair_copy().start()
    lax.fori_loop(0, blocks, weigh, 0)
    pair_copy().wait()
    part[...] = x_ref[...] + pairs[...]

    def send_part(p, carry):
        every_copy(p, chip).start()
        return carry

    lax.fori_loop(1, CHIPS, send_part, 0)
    every[chip] = part[...]
    share = 1.0 / jnp.sum(low[...], axis=0, keepdims=True)
    low[...] = jnp.broadcast_to(share, (8, ROWS))
    for g in range(GROUP):
        cols = slice(g * C, (g + 1) * C)
        at = slice(g * AD, (g + 1) * AD)
        attended = jnp.transpose(att[:, cols] * low[0:1, cols])
        opening = 1.0 / (1.0 + jnp.exp(-gate_ref[:, at].astype(f32)))
        cot = cot_ref[:, at].astype(f32)
        out_ref[:, at] = (attended * opening).astype(bf16)
        up = (cot * opening).astype(bf16)
        ups[cols, :] = up
        dgate_ref[:, at] = (cot * attended * opening * (1.0 - opening)).astype(bf16)
        center = jnp.sum(jnp.transpose(up.astype(f32) * attended), axis=0, keepdims=True)
        cent[:, cols] = jnp.broadcast_to(center, (8, C))

    def give_copy(c):
        return remote(give.at[c], got.at[c], g_send.at[c], g_recv.at[c], mate)

    def both_copy(c, source):
        return remote(both.at[c], taken.at[source], b_send.at[c], b_recv.at[source], 2 * c + core)

    def grads(kb):
        keys = kv_ref[rows_of(kb), 0:AD]
        values = kv_ref[rows_of(kb), AD : 2 * AD]
        dk = jnp.zeros((KB, AD), f32)
        dv = jnp.zeros((KB, AD), f32)
        for i in range(parts):
            cols = slice(i * width, (i + 1) * width)
            p = probs[rows_of(kb), cols] * low[0:1, cols]
            dp = lax.dot_general(values, ups[cols, :], NT, preferred_element_type=f32)
            ds = (p * (dp - cent[0:1, cols])).astype(bf16)
            dv = dv + lax.dot_general(p.astype(bf16), ups[cols, :], NN, preferred_element_type=f32)
            dk = dk + lax.dot_general(ds, qs[cols, :], NN, preferred_element_type=f32)
            dqt[:, cols] = dqt[:, cols] + lax.dot_general(
                keys, ds, TN, preferred_element_type=f32
            )
        block[:, 0:AD] = dk
        block[:, AD : 2 * AD] = dv
        for u in range(KB // (2 * C)):
            c = kb * (KB // (2 * C)) + u
            mine = pl.multiple_of((2 * u + core) * C, C)
            theirs = pl.multiple_of((2 * u + 1 - core) * C, C)
            keep[c] = block[pl.ds(mine, C), :]
            give[c] = block[pl.ds(theirs, C), :].astype(bf16)

            @pl.when(c <= chip)
            def _():
                give_copy(c).start()

    def forward(kb):
        for u in range(KB // (2 * C)):
            c = kb * (KB // (2 * C)) + u

            @pl.when(c <= chip)
            def _():
                give_copy(c).wait_recv()
                both[c] = (keep[c] + got[c].astype(f32)).astype(bf16)

            @pl.when(c < chip)
            def _():
                both_copy(c, chip).start()

    def later(t, carry):
        kb = blocks - 1 - t
        grads(kb)
        forward(kb + 1)
        return carry

    grads(blocks - 1)
    lax.fori_loop(1, blocks, later, 0)
    forward(0)

    def take_part(p, carry):
        source = lax.rem(chip + p, CHIPS)
        every_copy(p, chip).wait_send()
        every_copy(p, source).wait_recv()
        return carry

    lax.fori_loop(1, CHIPS, take_part, 0)
    total[...] = jnp.sum(every[...], axis=0)
    for i in range(3):
        aside_copy(i).start()

    for g in range(GROUP):
        cols = slice(g * C, (g + 1) * C)
        dq_ref[:, g * AD : (g + 1) * AD] = (jnp.transpose(dqt[:, cols]) * scale).astype(bf16)

    keep[chip] = keep[chip] + got[chip].astype(f32)

    def collect(t, carry):
        source = CHIPS - 1 - t
        both_copy(source, source).wait_recv()
        keep[chip] = keep[chip] + taken[source].astype(f32)
        return carry

    def sent(c, carry):
        give_copy(c).wait_send()

        @pl.when(c < chip)
        def _():
            both_copy(c, chip).wait_send()

        return carry

    lax.fori_loop(0, CHIPS - 1 - chip, collect, 0)
    dk_ref[...] = keep[chip, :, 0:AD].astype(bf16)
    dv_ref[...] = keep[chip, :, AD : 2 * AD].astype(bf16)
    lax.fori_loop(0, chip + 1, sent, 0)
    for i in range(3):
        aside_copy(i).wait()
    same = slice(0, HEADS)
    gain = slice(HEADS, 2 * HEADS)
    sums_ref[same, :] = total[same, :] + others[0, same, :]
    sums_ref[gain, :] = (total[gain, :] + others[0, gain, :]) + (
        others[1, gain, :] + others[2, gain, :]
    )


VM = pl.BlockSpec(memory_space=pltpu.VMEM)


SM = pl.BlockSpec(memory_space=pltpu.SMEM)


def call(kernel, outs, args, scratch=(), collective=None):
    options = {"vmem_limit_bytes": VMEM_BIG}
    if collective is not None:
        options.update(collective_id=collective, has_side_effects=True)
    return pl.pallas_call(
        kernel,
        out_shape=tuple(jax.ShapeDtypeStruct(s, d) for s, d in outs),
        in_specs=[SM if x.ndim == 1 else VM for x in args],
        out_specs=tuple(VM for _ in outs),
        scratch_shapes=list(scratch),
        compiler_params=pltpu.CompilerParams(**options),
    )(*args)


SQ = (HEADS, DK, DK)


def per_device(
    delta_query, delta_key, delta_value, beta_logit, decay_input, decay_log, norm_gain,
    output_gate, delta_cotangent, attn_query, attn_key, attn_value, attn_gate, attn_cotangent,
):
    q, k, v = delta_query[0], delta_key[0], delta_value[0]
    gates = (beta_logit[0].T, decay_input[0].T, decay_log)
    wide = (C, HEADS * DK)
    rows = (HEADS, C)
    pair = (2 * HEADS, DK)
    states = (N, SROWS, DK)

    def vm(shape, dtype=f32):
        return pltpu.VMEM(shape, dtype)

    def dma(count):
        return pltpu.SemaphoreType.DMA((count,))

    kv = jnp.concatenate([attn_key[0], attn_value[0]], axis=-1)
    kv_all = lax.all_gather(kv, "ctx", axis=0, tiled=True)

    inv, w, u0, m, off = call(
        chunk_kernel,
        [(SQ, f32), (SQ, f32), (SQ, f32), (SQ, bf16), ((N, SROWS + KEEP, DK), bf16)],
        (k, v) + gates,
    )
    m_all, keep_all, state = call(
        forward_exchange,
        [((N, DK, DK), bf16), ((N, 8, DK), f32), (states, bf16)],
        (m, off),
        [vm((N, SROWS + KEEP, DK), bf16), vm(states, bf16)] + [dma(N)] * 8,
        collective=1,
    )
    state = state.reshape(SQ)
    out, dgate, dgain, u, do, dul, dsl = call(
        output_kernel,
        [(wide, bf16), (wide, bf16), ((1, DK), f32), (SQ, f32), (SQ, f32), (SQ, f32), (SQ, bf16)],
        (state, q, k, w, u0) + gates + (norm_gain[None], output_gate[0], delta_cotangent[0]),
    )
    (dstate,) = call(
        backward_exchange,
        [(states, bf16)],
        (m_all, keep_all, dsl.reshape(states)),
        [vm(states, bf16), vm(states, bf16)] + [dma(N)] * 4,
        collective=2,
    )
    dq, dk, dv, dbl, ddi, sums = call(
        gradient_kernel,
        [(wide, bf16), (wide, bf16), (wide, bf16), (rows, f32), (rows, f32), (pair, f32)],
        (state, dstate.reshape(SQ), q, k, v, inv, u, do, dul) + gates + (dgain,),
    )
    flat = (C, GROUP * AD)
    own = (C, AD)
    blocks = (CHIPS, C, 2 * AD)
    attn_out, attn_dq, attn_dgate, attn_dk, attn_dv, sums = call(
        attention_kernel,
        [(flat, bf16), (flat, bf16), (flat, bf16), (own, bf16), (own, bf16), (pair, f32)],
        (attn_query[0], attn_gate[0], attn_cotangent[0], kv_all, sums),
        [
            vm((ROWS, AD), bf16), vm((ROWS, AD), bf16), vm((LENGTH, ROWS)),
            vm((AD, ROWS)), vm((AD, ROWS)), vm((8, ROWS)), vm((8, ROWS)), vm((8, ROWS)),
            vm((KB, 2 * AD)), vm(blocks), vm(blocks, bf16), vm(blocks, bf16),
            vm(blocks, bf16), vm(blocks, bf16),
            vm(pair), vm(pair), vm((CHIPS,) + pair), vm(pair), vm((3,) + pair),
        ]
        + [dma(CHIPS)] * 4
        + [pltpu.SemaphoreType.DMA] * 2
        + [dma(CHIPS)] * 2
        + [dma(3)] * 2,
        collective=3,
    )
    return (
        out[None], dq[None], dk[None], dv[None], dbl.T[None], ddi.T[None],
        sums[:HEADS, 0], sums[HEADS], dgate[None], attn_out[None], attn_dq[None],
        attn_dk[None], attn_dv[None], attn_dgate[None],
    )


def solution(mesh):
    split3 = P("section", "ctx", "head")
    in_specs = (split3,) * 5 + (P("head"), P()) + (split3,) * 7
    out_specs = (split3,) * 6 + (P("head"), P()) + (split3,) * 6
    return jax.shard_map(
        per_device, mesh=mesh, in_specs=in_specs, out_specs=out_specs, check_vma=False
    )
```

```python
import functools

import jax
import jax.numpy as jnp
from jax import lax
from jax.experimental import pallas as pl
from jax.experimental.pallas import tpu as pltpu
from jax.sharding import PartitionSpec as P

f32, bf16 = jnp.float32, jnp.bfloat16
MESH = pl.DeviceIdType.MESH
HIGHEST = lax.Precision.HIGHEST
NEG_FILL = -1e30
N = 32
C = 128
DK = 128
AD = 256
HEADS = 8
GROUP = 8
ROWS = GROUP * C
KB = 512
LENGTH = N * C
NKB = LENGTH // KB
QUARTERS = N // HEADS
SROWS = DK // QUARTERS
KEEP = 16
CHIPS = N // 2
VMEM_BIG = 60 * 1024 * 1024

NT = (((1,), (1,)), ((), ()))
NN = (((1,), (0,)), ((), ()))
TN = (((0,), (0,)), ((), ()))


def d1(a, b, dims):
    return lax.dot_general(a.astype(bf16), b.astype(bf16), dims, preferred_element_type=f32)


def split(a):
    hi = a.astype(bf16)
    return hi, (a - hi.astype(f32)).astype(bf16)


def d3(a, b, dims):
    ah, al = split(a)
    bh, bl = split(b)

    def dot(x, y):
        return lax.dot_general(x, y, dims, preferred_element_type=f32)

    return dot(ah, bh) + (dot(ah, bl) + dot(al, bh))


def dfull(a, b, dims):
    return lax.dot_general(a, b, dims, precision=HIGHEST, preferred_element_type=f32)


def iotas(shape=(C, C)):
    return (
        lax.broadcasted_iota(jnp.int32, shape, 0),
        lax.broadcasted_iota(jnp.int32, shape, 1),
    )


def unit(x):
    r = lax.rsqrt(jnp.sum(x * x, axis=-1, keepdims=True) + 1e-6)
    return x * r, r


def gates_of(bl_ref, di_ref, dl_ref):
    beta = 1.0 / (1.0 + jnp.exp(-bl_ref[...]))
    a = di_ref[...]
    head = lax.broadcasted_iota(jnp.int32, a.shape, 0)
    logs = jnp.zeros(a.shape, f32)
    for h in range(HEADS):
        logs = jnp.where(head == h, dl_ref[h], logs)
    rate = -jnp.exp(logs)
    soft = jnp.maximum(a, 0.0) + jnp.log1p(jnp.exp(-jnp.abs(a)))
    g = jnp.maximum(rate * soft, -104.0)
    r, c = iotas()
    beta_cols = dfull(jnp.where(r == c, 1.0, 0.0), beta, NT)
    cols = dfull(jnp.where(r >= c, 1.0, 0.0), g, NT)
    rows = dfull(g, jnp.where(r <= c, 1.0, 0.0), NN)
    return beta, g, rate, beta_cols, cols, rows


def fade(cc, cr):
    r, c = iotas()
    return jnp.where(r >= c, jnp.exp(jnp.where(r >= c, cc - cr, 0.0)), 0.0)


def head_cols(ref, h):
    return ref[:, h * DK : (h + 1) * DK].astype(f32)


def peers_of(me):
    core = lax.rem(me, 2)
    return me // 2, core, me + 1 - 2 * core


def remote(src, dst, send, recv, peer):
    if not isinstance(peer, dict):
        peer = {"ctx": peer}
    return pltpu.make_async_remote_copy(
        src_ref=src, dst_ref=dst, send_sem=send, recv_sem=recv, device_id=peer, device_id_type=MESH
    )


def whole_kernel(
    q_ref, k_ref, v_ref, bl_ref, di_ref, dl_ref, gain_ref, gate_ref, cot_ref,
    aq_ref, ak_ref, av_ref, ag_ref, ac_ref,
    out_ref, dq_ref, dk_ref, dv_ref, dbl_ref, ddi_ref, dgate_ref,
    aout_ref, adq_ref, adk_ref, adv_ref, adgate_ref, sums_ref,
    beta_s, cols_s, rows_s, n_ref, w_ref, u0_ref, u_ref, do_ref, dul_ref,
    m_ref, o_ref, mall, oall, eall, sbuf, srecv, l_ref, lall, tbuf, trecv,
    keys, values,
    qs, ups, probs, att, dqt, top, low, cent, block, keep, give, got, both, taken,
    x_ref, pairs, part, every, total, others,
    m_send, m_recv, f_send, f_recv, o_send, o_recv, s_send, s_recv, l_send, l_recv, t_send, t_recv,
    k_send, k_recv, kf_send, kf_recv, v_send, v_recv, vf_send, vf_recv,
    g_send, g_recv, b_send, b_recv, p_send, p_recv, e_send, e_recv, a_send, a_recv,
):
    me, head, section = (lax.axis_index(a) for a in ("ctx", "head", "section"))
    chip, core, mate = peers_of(me)
    barrier = pltpu.get_barrier_semaphore()
    turns = ((0, 1), (1, 0), (1, 1))

    def aside(i):
        dh, ds = turns[i]
        return {"head": lax.rem(head + dh, 2), "section": lax.rem(section + ds, 2)}

    def hello(p, carry):
        pl.semaphore_signal(
            barrier, inc=1, device_id={"ctx": lax.rem(me + p, N)}, device_id_type=MESH
        )
        return carry

    lax.fori_loop(1, N, hello, 0)
    for i in range(3):
        pl.semaphore_signal(barrier, inc=1, device_id=aside(i), device_id_type=MESH)

    r, c = iotas()
    beta_rows, g, rate, beta, cols, rows = gates_of(bl_ref, di_ref, dl_ref)
    beta_s[...] = beta
    cols_s[...] = cols
    rows_s[...] = rows

    def chunk(heads):
        ks = [unit(head_cols(k_ref, h))[0] for h in heads]
        lows = []
        for h, K in zip(heads, ks):
            F = fade(cols[:, h : h + 1], rows[h : h + 1, :])
            lows.append(jnp.where(r > c, beta[:, h : h + 1] * F * d1(K, K, NT), 0.0))
        inv = [
            jnp.where(r == c, 1.0, 0.0) - jnp.where(r // 2 == c // 2, L, 0.0) for L in lows
        ]
        k = 2
        while k < C:
            part_k = (r // (2 * k) == c // (2 * k)) & (r // k != c // k)
            mid = [d1(I, jnp.where(part_k, L, 0.0), NN) for I, L in zip(inv, lows)]
            inv = [I - d1(T, I, NN) for I, T in zip(inv, mid)]
            k *= 2
        for h, K, I in zip(heads, ks, inv):
            b, cc = beta[:, h : h + 1], cols[:, h : h + 1]
            V = head_cols(v_ref, h)
            W = d3(I, (b * jnp.exp(cc)) * K, NN)
            U0 = d3(I, b * V, NN)
            cl = cc[C - 1 : C, :]
            Kt = jnp.exp(cl - cc) * K
            n_ref[h] = I
            w_ref[h] = W
            u0_ref[h] = U0
            m_ref[h] = (-d3(W, Kt, TN)).astype(bf16)
            off = d3(U0, Kt, TN).astype(bf16)
            stay = jnp.broadcast_to(jnp.exp(cl), (KEEP, DK))
            high = stay.astype(bf16)
            mid = (stay - high.astype(f32)).astype(bf16)
            last = stay - high.astype(f32) - mid.astype(f32)
            row = lax.broadcasted_iota(jnp.int32, (KEEP, DK), 0)
            terms = jnp.where(row == 0, high.astype(f32), jnp.where(row == 1, mid.astype(f32), last))
            for q in range(QUARTERS):
                o_ref[h * QUARTERS + q, 0:SROWS, :] = off[q * SROWS : (q + 1) * SROWS, :]
                o_ref[h * QUARTERS + q, SROWS : SROWS + KEEP, :] = terms.astype(bf16)

    def map_copy(peer, source):
        return remote(
            m_ref.at[peer // QUARTERS], mall.at[source], m_send.at[peer // 2], m_recv.at[source], peer
        )

    def offset_copy(peer, source):
        return remote(o_ref.at[peer], oall.at[source], o_send.at[peer], o_recv.at[source], peer)

    half = CHIPS // 2
    for first in (0, 1):
        chunk(range(first * HEADS // 2, (first + 1) * HEADS // 2))
        if first == 0:
            pl.semaphore_wait(barrier, N + 2)

        def send_map(t, carry):
            to = first * half + lax.rem(chip + t, half)

            @pl.when(to != chip)
            def _():
                map_copy(2 * to + core, me).start()

            return carry

        def send_offset(t, carry):
            to = first * N // 2 + lax.rem(me + t, N // 2)

            @pl.when(to != me)
            def _():
                offset_copy(to, me).start()

            return carry

        lax.fori_loop(0, half, send_map, 0)
        lax.fori_loop(0, N // 2, send_offset, 0)
    mall[me] = m_ref[me // QUARTERS]
    oall[me] = o_ref[me]

    def map_pass(source):
        return remote(mall.at[source], mall.at[source], f_send.at[source], f_recv.at[source], mate)

    def state_copy(s, source):
        return remote(sbuf.at[s], srecv.at[source], s_send.at[s], s_recv.at[source], s)

    def arrive(cc):
        source = 2 * cc + core

        @pl.when(source != me)
        def _():
            map_copy(source, source).wait_recv()

        map_pass(source).start()

    def advance(s, S):
        @pl.when(s != me)
        def _():
            offset_copy(s, s).wait_recv()

        sbuf[s] = S.astype(bf16)

        @pl.when(s != me)
        def _():
            state_copy(s, me).start()

        terms = oall[s, SROWS : SROWS + KEEP, :].astype(f32)
        stay = terms[0:1] + (terms[1:2] + terms[2:3])
        eall[s] = jnp.broadcast_to(stay, (8, DK))
        return stay * S + d1(S, mall[s], NN) + oall[s, 0:SROWS, :].astype(f32)

    def pair(cc, S):
        map_pass(2 * cc + 1 - core).wait_recv()
        return advance(2 * cc + 1, advance(2 * cc, S))

    def forth(cc, S):
        arrive(cc)
        return pair(cc - 1, S)

    arrive(0)
    S_end = lax.fori_loop(1, CHIPS, forth, jnp.zeros((SROWS, DK), f32))
    pair(CHIPS - 1, S_end)
    srecv[me] = sbuf[me]

    def take_state(p, carry):
        peer = lax.rem(me + p, N)
        state_copy(peer, peer).wait_recv()
        return carry

    lax.fori_loop(1, N, take_state, 0)

    def own_rows(device):
        return pl.ds(pl.multiple_of(device * C, C), C)

    def wide_copy(ref, send, recv, to, source):
        at = own_rows(2 * source + core)
        return remote(ref.at[at, :], ref.at[at, :], send.at[to], recv.at[source], 2 * to + core)

    def wide_pass(ref, send, recv, which, source):
        at = own_rows(2 * source + which)
        return remote(ref.at[at, :], ref.at[at, :], send.at[source], recv.at[source], mate)

    def spread(own, ref, send, recv):
        ref[own_rows(me), :] = own[...]

        @pl.when(lax.rem(chip, 2) == 0)
        def _():
            ref[pl.ds(pl.multiple_of((chip + 1) * 2 * C, C), 2 * C), :] = jnp.zeros((2 * C, AD), bf16)

        def go(to, carry):
            wide_copy(ref, send, recv, to, chip).start()
            return carry

        lax.fori_loop(chip + 1, CHIPS, go, 0)

    def pass_on(ref, send, recv, pass_send, pass_recv):
        wide_pass(ref, pass_send, pass_recv, core, chip).start()

        def go(t, carry):
            source = chip - t
            wide_copy(ref, send, recv, source, source).wait_recv()
            wide_pass(ref, pass_send, pass_recv, core, source).start()
            return carry

        lax.fori_loop(1, chip + 1, go, 0)

    def complete(ref, pass_send, pass_recv):
        def go(source, carry):
            wide_pass(ref, pass_send, pass_recv, 1 - core, source).wait_recv()
            return carry

        lax.fori_loop(0, chip + 1, go, 0)

    spread(ak_ref, keys, k_send, k_recv)

    def slope_copy(peer, source):
        return remote(l_ref.at[peer], lall.at[source], l_send.at[peer], l_recv.at[source], peer)

    def state_of(ref, h):
        return ref[h * QUARTERS : (h + 1) * QUARTERS].reshape(DK, DK).astype(f32)

    gain = gain_ref[...]
    gain_sum = jnp.zeros((1, DK), f32)
    for h in range(HEADS):
        at = slice(h * DK, (h + 1) * DK)
        Q = unit(head_cols(q_ref, h))[0] * DK**-0.5
        K = unit(head_cols(k_ref, h))[0]
        S, W = state_of(srecv, h), w_ref[h]
        cc = cols_s[:, h : h + 1]
        ec = jnp.exp(cc)
        F = fade(cc, rows_s[h : h + 1, :])
        U = u0_ref[h] - d3(W, S, NT)
        Pm = d3(Q, K, NT) * F
        m = ec * d3(Q, S, NT) + d3(Pm, U, NN)
        rr = lax.rsqrt(jnp.mean(m * m, axis=-1, keepdims=True) + 1e-6)
        gate = head_cols(gate_ref, h)
        cot = head_cols(cot_ref, h)
        sig = 1.0 / (1.0 + jnp.exp(-gate))
        silu = gate * sig
        nm = m * rr
        out_ref[:, at] = (nm * gain * silu).astype(bf16)
        dgate_ref[:, at] = (cot * nm * gain * (sig * (1.0 + gate * (1.0 - sig)))).astype(bf16)
        gain_sum = gain_sum + jnp.sum(cot * nm * silu, axis=0, keepdims=True)
        dn = cot * gain * silu
        dO = rr * dn - m * (rr * rr * rr) * jnp.mean(m * dn, axis=-1, keepdims=True)
        dUl = d3(Pm, dO, TN)
        u_ref[h] = U
        do_ref[h] = dO
        dul_ref[h] = dUl
        slope = (d3(ec * dO, Q, TN) - d3(dUl, W, TN)).astype(bf16)
        for q in range(QUARTERS):
            l_ref[h * QUARTERS + q] = slope[q * SROWS : (q + 1) * SROWS, :]

    x_ref[HEADS : 2 * HEADS, :] = jnp.broadcast_to(gain_sum, (HEADS, DK))

    def send_slope(p, carry):
        slope_copy(lax.rem(me + p, N), me).start()
        return carry

    lax.fori_loop(1, N, send_slope, 0)
    lall[me] = l_ref[me]

    def turn_copy(s, source):
        return remote(tbuf.at[s], trecv.at[source], t_send.at[s], t_recv.at[source], s)

    def back(t, S):
        s = N - 1 - t
        tbuf[s] = S.astype(bf16)

        @pl.when(s != me)
        def _():
            turn_copy(s, me).start()
            slope_copy(s, s).wait_recv()

        return eall[s, 0:1, :] * S + d1(S, mall[s], NT) + lall[s].astype(f32)

    lax.fori_loop(0, N, back, jnp.zeros((SROWS, DK), f32))
    trecv[me] = tbuf[me]
    pass_on(keys, k_send, k_recv, kf_send, kf_recv)

    def take_turn(p, carry):
        peer = lax.rem(me + p, N)
        turn_copy(peer, peer).wait_recv()
        return carry

    lax.fori_loop(1, N, take_turn, 0)
    spread(av_ref, values, v_send, v_recv)

    lane = lax.broadcasted_iota(jnp.int32, (C, DK), 1)
    sub = lax.broadcasted_iota(jnp.int32, (HEADS, C), 0)
    dbeta = jnp.zeros((C, DK), f32)
    dcol = jnp.zeros((C, DK), f32)
    drow = jnp.zeros((HEADS, C), f32)
    dlast = jnp.zeros((HEADS, C), f32)
    for h in range(HEADS):
        at = slice(h * DK, (h + 1) * DK)
        xq, xk = head_cols(q_ref, h), head_cols(k_ref, h)
        Q0, rq = unit(xq)
        Q = Q0 * DK**-0.5
        K, rk = unit(xk)
        V = head_cols(v_ref, h)
        S, dS = state_of(srecv, h), state_of(trecv, h)
        I, U, dO, dUl = n_ref[h], u_ref[h], do_ref[h], dul_ref[h]
        b, cc = beta_s[:, h : h + 1], cols_s[:, h : h + 1]
        ec = jnp.exp(cc)
        F = fade(cc, rows_s[h : h + 1, :])
        cl = cc[C - 1 : C, :]
        tail = jnp.exp(cl - cc)
        A = d1(K, K, NT)
        QK = d3(Q, K, NT)
        dU = dUl + d3(tail * K, dS, NT)
        QS = ec * d3(Q, S, NT)
        Y = d3(K, S, NT)
        dPF = d3(dO, U, NT) * F
        dQ = ec * d3(dO, S, NN) + d3(dPF, K, NN)
        dKt = tail * d3(U, dS, NN)
        tau = jnp.sum(dKt * K, axis=-1, keepdims=True)
        dcl = jnp.sum(tau, axis=0, keepdims=True) + jnp.exp(cl) * jnp.sum(
            jnp.sum(dS * S, axis=-1, keepdims=True), axis=0, keepdims=True
        )
        dR = d3(I, dU, TN)
        dV = b * dR
        dY = (-ec) * dV
        dLF = jnp.where(r > c, -d3(dR, U, NT), 0.0) * F
        G2 = dLF * A
        db = jnp.sum(dR * (V - ec * Y), axis=-1, keepdims=True) + jnp.sum(
            G2, axis=-1, keepdims=True
        )
        dA = b * dLF
        dK = d3(dPF, Q, TN) + dKt + d3(dY, S, NN) + d3(dA, K, NN) + d3(dA, K, TN)
        G = dPF * QK + b * G2
        dcc = jnp.sum(dO * QS + dY * Y, axis=-1, keepdims=True) - tau + jnp.sum(
            G, axis=-1, keepdims=True
        )
        dbeta = jnp.where(lane == h, db, dbeta)
        dcol = jnp.where(lane == h, dcc, dcol)
        drow = jnp.where(sub == h, -jnp.sum(G, axis=0, keepdims=True), drow)
        dlast = jnp.where(sub == h, dcl, dlast)
        dq_ref[:, at] = (
            DK**-0.5 * (rq * dQ - xq * (rq * rq * rq) * jnp.sum(xq * dQ, axis=-1, keepdims=True))
        ).astype(bf16)
        dk_ref[:, at] = (
            rk * dK - xk * (rk * rk * rk) * jnp.sum(xk * dK, axis=-1, keepdims=True)
        ).astype(bf16)
        dv_ref[:, at] = dV.astype(bf16)
    since = jnp.where(r >= c, 1.0, 0.0)
    dg = dfull(dcol, since, TN)[:HEADS] + dfull(drow, since, NN) + dlast
    dbeta = dfull(dbeta, jnp.where(r == c, 1.0, 0.0), TN)[:HEADS]
    dbl_ref[...] = dbeta * beta_rows * (1.0 - beta_rows)
    ddi_ref[...] = dg * rate / (1.0 + jnp.exp(-di_ref[...]))
    x_ref[0:HEADS, :] = jnp.zeros((HEADS, DK), f32)
    x_ref[0:HEADS, 0:HEADS] = dfull(jnp.ones((HEADS, C), f32), dg * g, NT)

    def pair_copy():
        return remote(x_ref, pairs, p_send, p_recv, mate)

    def every_copy(p, source):
        peer = lax.rem(chip + p, CHIPS) * 2 + core
        return remote(part, every.at[source], e_send.at[p], e_recv.at[source], peer)

    def aside_copy(i):
        return remote(total, others.at[i], a_send.at[i], a_recv.at[i], aside(i))

    pair_copy().start()
    pass_on(values, v_send, v_recv, vf_send, vf_recv)
    blocks = me // (KB // C) + 1
    scale = AD**-0.5
    width = 256
    parts = ROWS // width
    for g in range(GROUP):
        qs[g * C : (g + 1) * C, :] = (
            aq_ref[:, g * AD : (g + 1) * AD].astype(f32) * scale
        ).astype(bf16)
    top[...] = jnp.full((8, ROWS), NEG_FILL, f32)
    low[...] = jnp.zeros((8, ROWS), f32)
    att[...] = jnp.zeros((AD, ROWS), f32)
    dqt[...] = jnp.zeros((AD, ROWS), f32)
    key_at, query_at = iotas((KB, width))
    reach = me * C + lax.rem(query_at, C) - key_at

    def rows_of(kb):
        return pl.ds(pl.multiple_of(kb * KB, KB), KB)

    def score(kb, carry):
        kblock = keys[rows_of(kb), :]
        for i in range(parts):
            cols = slice(i * width, (i + 1) * width)
            s = lax.dot_general(kblock, qs[cols, :], NT, preferred_element_type=f32)
            s = jnp.where(reach >= kb * KB, s, NEG_FILL)
            probs[rows_of(kb), cols] = s
            top[:, cols] = jnp.maximum(
                top[:, cols], jnp.max(s.reshape(KB // 8, 8, width), axis=0)
            )
        return carry

    complete(keys, kf_send, kf_recv)
    lax.fori_loop(0, blocks, score, 0)
    peak = jnp.max(top[...], axis=0, keepdims=True)
    top[...] = jnp.broadcast_to(peak, (8, ROWS))

    def weigh(kb, carry):
        vblock = values[rows_of(kb), :]
        for i in range(parts):
            cols = slice(i * width, (i + 1) * width)
            p = jnp.exp(probs[rows_of(kb), cols] - top[0:1, cols])
            probs[rows_of(kb), cols] = p
            low[:, cols] = low[:, cols] + jnp.sum(p.reshape(KB // 8, 8, width), axis=0)
            att[:, cols] = att[:, cols] + lax.dot_general(
                vblock, p.astype(bf16), TN, preferred_element_type=f32
            )
        return carry

    pair_copy().wait()
    part[...] = x_ref[...] + pairs[...]

    def send_part(p, carry):
        every_copy(p, chip).start()
        return carry

    lax.fori_loop(1, CHIPS, send_part, 0)
    every[chip] = part[...]
    complete(values, vf_send, vf_recv)
    lax.fori_loop(0, blocks, weigh, 0)
    share = 1.0 / jnp.sum(low[...], axis=0, keepdims=True)
    low[...] = jnp.broadcast_to(share, (8, ROWS))
    for g in range(GROUP):
        cols = slice(g * C, (g + 1) * C)
        at = slice(g * AD, (g + 1) * AD)
        attended = jnp.transpose(att[:, cols] * low[0:1, cols])
        opening = 1.0 / (1.0 + jnp.exp(-ag_ref[:, at].astype(f32)))
        cot = ac_ref[:, at].astype(f32)
        aout_ref[:, at] = (attended * opening).astype(bf16)
        up = (cot * opening).astype(bf16)
        ups[cols, :] = up
        adgate_ref[:, at] = (cot * attended * opening * (1.0 - opening)).astype(bf16)
        center = jnp.sum(jnp.transpose(up.astype(f32) * attended), axis=0, keepdims=True)
        cent[:, cols] = jnp.broadcast_to(center, (8, C))

    def give_copy(c):
        return remote(give.at[c], got.at[c], g_send.at[c], g_recv.at[c], mate)

    def both_copy(c, source):
        return remote(both.at[c], taken.at[source], b_send.at[c], b_recv.at[source], 2 * c + core)

    def grads(kb):
        kblock = keys[rows_of(kb), :]
        vblock = values[rows_of(kb), :]
        dk = jnp.zeros((KB, AD), f32)
        dv = jnp.zeros((KB, AD), f32)
        for i in range(parts):
            cols = slice(i * width, (i + 1) * width)
            p = probs[rows_of(kb), cols] * low[0:1, cols]
            dp = lax.dot_general(vblock, ups[cols, :], NT, preferred_element_type=f32)
            ds = (p * (dp - cent[0:1, cols])).astype(bf16)
            dv = dv + lax.dot_general(p.astype(bf16), ups[cols, :], NN, preferred_element_type=f32)
            dk = dk + lax.dot_general(ds, qs[cols, :], NN, preferred_element_type=f32)
            dqt[:, cols] = dqt[:, cols] + lax.dot_general(
                kblock, ds, TN, preferred_element_type=f32
            )
        block[:, 0:AD] = dk
        block[:, AD : 2 * AD] = dv
        for u in range(KB // (2 * C)):
            c = kb * (KB // (2 * C)) + u
            mine = pl.multiple_of((2 * u + core) * C, C)
            theirs = pl.multiple_of((2 * u + 1 - core) * C, C)
            keep[c] = block[pl.ds(mine, C), :]
            give[c] = block[pl.ds(theirs, C), :].astype(bf16)

            @pl.when(c <= chip)
            def _():
                give_copy(c).start()

    def forward(kb):
        for u in range(KB // (2 * C)):
            c = kb * (KB // (2 * C)) + u

            @pl.when(c <= chip)
            def _():
                give_copy(c).wait_recv()
                both[c] = (keep[c] + got[c].astype(f32)).astype(bf16)

            @pl.when(c < chip)
            def _():
                both_copy(c, chip).start()

    def later(t, carry):
        kb = blocks - 1 - t
        grads(kb)
        forward(kb + 1)
        return carry

    grads(blocks - 1)
    lax.fori_loop(1, blocks, later, 0)
    forward(0)

    def take_part(p, carry):
        source = lax.rem(chip + p, CHIPS)
        every_copy(p, chip).wait_send()
        every_copy(p, source).wait_recv()
        return carry

    lax.fori_loop(1, CHIPS, take_part, 0)
    total[...] = jnp.sum(every[...], axis=0)
    for i in range(3):
        aside_copy(i).start()

    for g in range(GROUP):
        cols = slice(g * C, (g + 1) * C)
        adq_ref[:, g * AD : (g + 1) * AD] = (jnp.transpose(dqt[:, cols]) * scale).astype(bf16)

    keep[chip] = keep[chip] + got[chip].astype(f32)

    def collect(t, carry):
        source = CHIPS - 1 - t
        both_copy(source, source).wait_recv()
        keep[chip] = keep[chip] + taken[source].astype(f32)
        return carry

    def sent(c, carry):
        give_copy(c).wait_send()

        @pl.when(c < chip)
        def _():
            both_copy(c, chip).wait_send()

        return carry

    lax.fori_loop(0, CHIPS - 1 - chip, collect, 0)
    adk_ref[...] = keep[chip, :, 0:AD].astype(bf16)
    adv_ref[...] = keep[chip, :, AD : 2 * AD].astype(bf16)
    lax.fori_loop(0, chip + 1, sent, 0)
    for i in range(3):
        aside_copy(i).wait()
    same = slice(0, HEADS)
    gain = slice(HEADS, 2 * HEADS)
    sums_ref[same, :] = total[same, :] + others[0, same, :]
    sums_ref[gain, :] = (total[gain, :] + others[0, gain, :]) + (
        others[1, gain, :] + others[2, gain, :]
    )

    def drain(p, carry):
        peer = lax.rem(me + p, N)
        offset_copy(peer, me).wait_send()
        state_copy(peer, me).wait_send()
        slope_copy(peer, me).wait_send()
        turn_copy(peer, me).wait_send()
        return carry

    def drain_map(p, carry):
        map_copy(lax.rem(chip + p, CHIPS) * 2 + core, me).wait_send()
        return carry

    def drain_pass(cc, carry):
        map_pass(2 * cc + core).wait_send()
        return carry

    def drain_wide(to, carry):
        wide_copy(keys, k_send, k_recv, to, chip).wait_send()
        wide_copy(values, v_send, v_recv, to, chip).wait_send()
        return carry

    def drain_wide_pass(source, carry):
        wide_pass(keys, kf_send, kf_recv, core, source).wait_send()
        wide_pass(values, vf_send, vf_recv, core, source).wait_send()
        return carry

    lax.fori_loop(1, N, drain, 0)
    lax.fori_loop(1, CHIPS, drain_map, 0)
    lax.fori_loop(0, CHIPS, drain_pass, 0)
    lax.fori_loop(chip + 1, CHIPS, drain_wide, 0)
    lax.fori_loop(0, chip + 1, drain_wide_pass, 0)


def place_kernel(count, sums_ref, *refs):
    ins, outs = refs[:count], refs[count : 2 * count]
    log_ref, gain_ref, sems = refs[2 * count :]
    copies = [pltpu.make_async_copy(a, b, sems.at[i]) for i, (a, b) in enumerate(zip(ins, outs))]
    for copy in copies:
        copy.start()
    log_ref[...] = sums_ref[0:1, 0:HEADS]
    gain_ref[...] = sums_ref[HEADS : HEADS + 1, :]
    for copy in copies:
        copy.wait()


VM = pl.BlockSpec(memory_space=pltpu.VMEM)
SM = pl.BlockSpec(memory_space=pltpu.SMEM)
ANY = pl.BlockSpec(memory_space=pl.ANY)


def per_device(
    delta_query, delta_key, delta_value, beta_logit, decay_input, decay_log, norm_gain,
    output_gate, delta_cotangent, attn_query, attn_key, attn_value, attn_gate, attn_cotangent,
):
    wide, flat, own = (C, HEADS * DK), (C, GROUP * AD), (C, AD)
    rows, pair = (HEADS, C), (2 * HEADS, DK)
    square, states = (HEADS, DK, DK), (N, SROWS, DK)
    loaded = (N, SROWS + KEEP, DK)
    blocks = (CHIPS, C, 2 * AD)
    args = (
        delta_query[0], delta_key[0], delta_value[0], beta_logit[0].T, decay_input[0].T, decay_log,
        norm_gain[None], output_gate[0], delta_cotangent[0],
        attn_query[0], attn_key[0], attn_value[0], attn_gate[0], attn_cotangent[0],
    )

    def vm(shape, dtype=f32):
        return pltpu.VMEM(shape, dtype)

    def dma(count):
        return pltpu.SemaphoreType.DMA((count,))

    one = pltpu.SemaphoreType.DMA
    shapes = [(wide, bf16)] * 4 + [(rows, f32)] * 2 + [(wide, bf16)]
    shapes += [(flat, bf16)] * 2 + [(own, bf16)] * 2 + [(flat, bf16), (pair, f32)]
    shapes = [jax.ShapeDtypeStruct(s, d) for s, d in shapes]
    results = pl.pallas_call(
        whole_kernel,
        out_shape=tuple(shapes),
        in_specs=[SM if x.ndim == 1 else VM for x in args],
        out_specs=tuple(VM for _ in shapes),
        scratch_shapes=[vm((C, HEADS)), vm((C, HEADS)), vm(rows)]
        + [vm(square)] * 6
        + [vm(square, bf16), vm(loaded, bf16), vm((N, DK, DK), bf16), vm(loaded, bf16)]
        + [vm((N, 8, DK))]
        + [vm(states, bf16)] * 6
        + [vm((LENGTH, AD), bf16)] * 2
        + [vm((ROWS, AD), bf16)] * 2
        + [vm((LENGTH, ROWS)), vm((AD, ROWS)), vm((AD, ROWS))]
        + [vm((8, ROWS))] * 3
        + [vm((KB, 2 * AD)), vm(blocks)]
        + [vm(blocks, bf16)] * 4
        + [vm(pair), vm(pair), vm(pair), vm((CHIPS,) + pair), vm(pair), vm((3,) + pair)]
        + [dma(N)] * 12
        + [dma(CHIPS)] * 12
        + [one, one]
        + [dma(CHIPS)] * 2
        + [dma(3)] * 2,
        compiler_params=pltpu.CompilerParams(
            vmem_limit_bytes=VMEM_BIG, collective_id=1, has_side_effects=True
        ),
    )(*args)
    results, sums = results[:-1], results[-1]
    count = len(results)
    *placed, log_grad, gain_grad = pl.pallas_call(
        functools.partial(place_kernel, count),
        out_shape=tuple(shapes[:-1])
        + (jax.ShapeDtypeStruct((1, HEADS), f32), jax.ShapeDtypeStruct((1, DK), f32)),
        in_specs=[VM] + [ANY] * count,
        out_specs=(VM,) * (count + 2),
        scratch_shapes=[dma(count)],
        compiler_params=pltpu.CompilerParams(vmem_limit_bytes=VMEM_BIG),
    )(sums, *results)
    out, dq, dk, dv, dbl, ddi, dgate, aout, adq, adk, adv, adgate = placed
    return (
        out[None], dq[None], dk[None], dv[None], dbl.T[None], ddi.T[None], log_grad[0], gain_grad[0],
        dgate[None], aout[None], adq[None], adk[None], adv[None], adgate[None],
    )


def solution(mesh):
    split3 = P("section", "ctx", "head")
    in_specs = (split3,) * 5 + (P("head"), P()) + (split3,) * 7
    out_specs = (split3,) * 6 + (P("head"), P()) + (split3,) * 6
    return jax.shard_map(
        per_device, mesh=mesh, in_specs=in_specs, out_specs=out_specs, check_vma=False
    )
```

```python
import functools

import jax
import jax.numpy as jnp
from jax import lax
from jax.experimental import pallas as pl
from jax.experimental.pallas import tpu as pltpu
from jax.sharding import PartitionSpec as P

f32, bf16 = jnp.float32, jnp.bfloat16
MESH = pl.DeviceIdType.MESH
HIGHEST = lax.Precision.HIGHEST
NEG_FILL = -1e30
N = 32
C = 128
DK = 128
AD = 256
HEADS = 8
GROUP = 8
ROWS = GROUP * C
KB = 512
LENGTH = N * C
NKB = LENGTH // KB
QUARTERS = N // HEADS
SROWS = DK // QUARTERS
KEEP = 16
CHIPS = N // 2
VMEM_BIG = 60 * 1024 * 1024

NT = (((1,), (1,)), ((), ()))
NN = (((1,), (0,)), ((), ()))
TN = (((0,), (0,)), ((), ()))


def d1(a, b, dims):
    return lax.dot_general(a.astype(bf16), b.astype(bf16), dims, preferred_element_type=f32)


def split(a):
    hi = a.astype(bf16)
    return hi, (a - hi.astype(f32)).astype(bf16)


def d3(a, b, dims):
    ah, al = split(a)
    bh, bl = split(b)

    def dot(x, y):
        return lax.dot_general(x, y, dims, preferred_element_type=f32)

    return dot(ah, bh) + (dot(ah, bl) + dot(al, bh))


def dfull(a, b, dims):
    return lax.dot_general(a, b, dims, precision=HIGHEST, preferred_element_type=f32)


def iotas(shape=(C, C)):
    return (
        lax.broadcasted_iota(jnp.int32, shape, 0),
        lax.broadcasted_iota(jnp.int32, shape, 1),
    )


def unit(x):
    r = lax.rsqrt(jnp.sum(x * x, axis=-1, keepdims=True) + 1e-6)
    return x * r, r


def gates_of(bl_ref, di_ref, dl_ref):
    beta = 1.0 / (1.0 + jnp.exp(-bl_ref[...]))
    a = di_ref[...]
    head = lax.broadcasted_iota(jnp.int32, a.shape, 0)
    logs = jnp.zeros(a.shape, f32)
    for h in range(HEADS):
        logs = jnp.where(head == h, dl_ref[h], logs)
    rate = -jnp.exp(logs)
    soft = jnp.maximum(a, 0.0) + jnp.log1p(jnp.exp(-jnp.abs(a)))
    g = jnp.maximum(rate * soft, -104.0)
    r, c = iotas()
    beta_cols = dfull(jnp.where(r == c, 1.0, 0.0), beta, NT)
    cols = dfull(jnp.where(r >= c, 1.0, 0.0), g, NT)
    rows = dfull(g, jnp.where(r <= c, 1.0, 0.0), NN)
    return beta, g, rate, beta_cols, cols, rows


def fade(cc, cr):
    r, c = iotas()
    return jnp.where(r >= c, jnp.exp(jnp.where(r >= c, cc - cr, 0.0)), 0.0)


def head_cols(ref, h):
    return ref[:, h * DK : (h + 1) * DK].astype(f32)


def peers_of(me):
    core = lax.rem(me, 2)
    return me // 2, core, me + 1 - 2 * core


def remote(src, dst, send, recv, peer):
    if not isinstance(peer, dict):
        peer = {"ctx": peer}
    return pltpu.make_async_remote_copy(
        src_ref=src, dst_ref=dst, send_sem=send, recv_sem=recv, device_id=peer, device_id_type=MESH
    )


def whole_kernel(
    q_ref, k_ref, v_ref, bl_ref, di_ref, dl_ref, gain_ref, gate_ref, cot_ref,
    aq_ref, ak_ref, av_ref, ag_ref, ac_ref,
    out_ref, dq_ref, dk_ref, dv_ref, dbl_ref, ddi_ref, dgate_ref,
    aout_ref, adq_ref, adk_ref, adv_ref, adgate_ref, sums_ref,
    beta_s, cols_s, rows_s, n_ref, w_ref, u0_ref, u_ref, do_ref, dul_ref,
    m_ref, o_ref, mall, oall, eall, sbuf, srecv, l_ref, lall, tbuf, trecv,
    keys, values,
    qs, ups, probs, att, dqt, top, low, cent, block, keep, give, got, both, taken,
    x_ref, pairs, part, every, total, others,
    m_send, m_recv, f_send, f_recv, o_send, o_recv, s_send, s_recv, l_send, l_recv, t_send, t_recv,
    k_send, k_recv, kf_send, kf_recv, v_send, v_recv, vf_send, vf_recv,
    g_send, g_recv, b_send, b_recv, p_send, p_recv, e_send, e_recv, a_send, a_recv,
):
    me, head, section = (lax.axis_index(a) for a in ("ctx", "head", "section"))
    chip, core, mate = peers_of(me)
    barrier = pltpu.get_barrier_semaphore()
    turns = ((0, 1), (1, 0), (1, 1))

    def aside(i):
        dh, ds = turns[i]
        return {"head": lax.rem(head + dh, 2), "section": lax.rem(section + ds, 2)}

    def hello(p, carry):
        pl.semaphore_signal(
            barrier, inc=1, device_id={"ctx": lax.rem(me + p, N)}, device_id_type=MESH
        )
        return carry

    lax.fori_loop(1, N, hello, 0)
    for i in range(3):
        pl.semaphore_signal(barrier, inc=1, device_id=aside(i), device_id_type=MESH)

    r, c = iotas()
    beta_rows, decay, rate, beta, cols, rows = gates_of(bl_ref, di_ref, dl_ref)
    beta_s[...] = beta
    cols_s[...] = cols
    rows_s[...] = rows

    def own_rows(device):
        return pl.ds(pl.multiple_of(device * C, C), C)

    def wide_copy(ref, send, recv, to, source):
        at = own_rows(2 * source + core)
        return remote(ref.at[at, :], ref.at[at, :], send.at[to], recv.at[source], 2 * to + core)

    def wide_pass(ref, send, recv, which, source):
        at = own_rows(2 * source + which)
        return remote(ref.at[at, :], ref.at[at, :], send.at[source], recv.at[source], mate)

    def spread(own, ref, send, recv):
        ref[own_rows(me), :] = own[...]

        @pl.when(lax.rem(chip, 2) == 0)
        def _():
            ref[pl.ds(pl.multiple_of((chip + 1) * 2 * C, C), 2 * C), :] = jnp.zeros((2 * C, AD), bf16)

        def go(to, carry):
            wide_copy(ref, send, recv, to, chip).start()
            return carry

        lax.fori_loop(chip + 1, CHIPS, go, 0)

    def pass_on(ref, send, recv, pass_send, pass_recv):
        wide_pass(ref, pass_send, pass_recv, core, chip).start()

        def go(t, carry):
            source = chip - t
            wide_copy(ref, send, recv, source, source).wait_recv()
            wide_pass(ref, pass_send, pass_recv, core, source).start()
            return carry

        lax.fori_loop(1, chip + 1, go, 0)

    def complete(ref, pass_send, pass_recv):
        def go(source, carry):
            wide_pass(ref, pass_send, pass_recv, 1 - core, source).wait_recv()
            return carry

        lax.fori_loop(0, chip + 1, go, 0)

    pl.semaphore_wait(barrier, N + 2)
    spread(ak_ref, keys, k_send, k_recv)

    def chunk(heads):
        ks = [unit(head_cols(k_ref, h))[0] for h in heads]
        lows = []
        for h, K in zip(heads, ks):
            F = fade(cols[:, h : h + 1], rows[h : h + 1, :])
            lows.append(jnp.where(r > c, beta[:, h : h + 1] * F * d1(K, K, NT), 0.0))
        inv = [
            jnp.where(r == c, 1.0, 0.0) - jnp.where(r // 2 == c // 2, L, 0.0) for L in lows
        ]
        k = 2
        while k < C:
            part_k = (r // (2 * k) == c // (2 * k)) & (r // k != c // k)
            mid = [d1(I, jnp.where(part_k, L, 0.0), NN) for I, L in zip(inv, lows)]
            inv = [I - d1(T, I, NN) for I, T in zip(inv, mid)]
            k *= 2
        for h, K, I in zip(heads, ks, inv):
            b, cc = beta[:, h : h + 1], cols[:, h : h + 1]
            V = head_cols(v_ref, h)
            W = d3(I, (b * jnp.exp(cc)) * K, NN)
            U0 = d3(I, b * V, NN)
            cl = cc[C - 1 : C, :]
            Kt = jnp.exp(cl - cc) * K
            n_ref[h] = I
            w_ref[h] = W
            u0_ref[h] = U0
            m_ref[h] = (-d3(W, Kt, TN)).astype(bf16)
            off = d3(U0, Kt, TN).astype(bf16)
            stay = jnp.broadcast_to(jnp.exp(cl), (KEEP, DK))
            high = stay.astype(bf16)
            mid = (stay - high.astype(f32)).astype(bf16)
            last = stay - high.astype(f32) - mid.astype(f32)
            row = lax.broadcasted_iota(jnp.int32, (KEEP, DK), 0)
            terms = jnp.where(row == 0, high.astype(f32), jnp.where(row == 1, mid.astype(f32), last))
            for q in range(QUARTERS):
                o_ref[h * QUARTERS + q, 0:SROWS, :] = off[q * SROWS : (q + 1) * SROWS, :]
                o_ref[h * QUARTERS + q, SROWS : SROWS + KEEP, :] = terms.astype(bf16)

    def map_copy(peer, source):
        return remote(
            m_ref.at[peer // QUARTERS], mall.at[source], m_send.at[peer // 2], m_recv.at[source], peer
        )

    def offset_copy(peer, source):
        return remote(o_ref.at[peer], oall.at[source], o_send.at[peer], o_recv.at[source], peer)

    half = CHIPS // 2
    for first in (0, 1):
        chunk(range(first * HEADS // 2, (first + 1) * HEADS // 2))
        def send_map(t, carry):
            to = first * half + lax.rem(chip + t, half)

            @pl.when(to != chip)
            def _():
                map_copy(2 * to + core, me).start()

            return carry

        def send_offset(t, carry):
            to = first * N // 2 + lax.rem(me + t, N // 2)

            @pl.when(to != me)
            def _():
                offset_copy(to, me).start()

            return carry

        lax.fori_loop(0, half, send_map, 0)
        lax.fori_loop(0, N // 2, send_offset, 0)
    mall[me] = m_ref[me // QUARTERS]
    oall[me] = o_ref[me]


    def map_pass(source):
        return remote(mall.at[source], mall.at[source], f_send.at[source], f_recv.at[source], mate)

    def state_copy(s, source):
        return remote(sbuf.at[s], srecv.at[source], s_send.at[s], s_recv.at[source], s)

    def arrive(cc):
        source = 2 * cc + core

        @pl.when(source != me)
        def _():
            map_copy(source, source).wait_recv()

        map_pass(source).start()

    def advance(s, S):
        @pl.when(s != me)
        def _():
            offset_copy(s, s).wait_recv()

        sbuf[s] = S.astype(bf16)

        @pl.when(s != me)
        def _():
            state_copy(s, me).start()

        terms = oall[s, SROWS : SROWS + KEEP, :].astype(f32)
        stay = terms[0:1] + (terms[1:2] + terms[2:3])
        eall[s] = jnp.broadcast_to(stay, (8, DK))
        return stay * S + d1(S, mall[s], NN) + oall[s, 0:SROWS, :].astype(f32)

    def pair(cc, S):
        map_pass(2 * cc + 1 - core).wait_recv()
        return advance(2 * cc + 1, advance(2 * cc, S))

    def forth(cc, S):
        arrive(cc)
        return pair(cc - 1, S)

    arrive(0)
    S_end = lax.fori_loop(1, CHIPS, forth, jnp.zeros((SROWS, DK), f32))
    pair(CHIPS - 1, S_end)
    srecv[me] = sbuf[me]

    spread(av_ref, values, v_send, v_recv)
    pass_on(keys, k_send, k_recv, kf_send, kf_recv)

    blocks = me // (KB // C) + 1
    scale = AD**-0.5
    width = 256
    parts = ROWS // width
    for g in range(GROUP):
        qs[g * C : (g + 1) * C, :] = (
            aq_ref[:, g * AD : (g + 1) * AD].astype(f32) * scale
        ).astype(bf16)
    top[...] = jnp.full((8, ROWS), NEG_FILL, f32)
    low[...] = jnp.zeros((8, ROWS), f32)
    att[...] = jnp.zeros((AD, ROWS), f32)
    dqt[...] = jnp.zeros((AD, ROWS), f32)
    key_at, query_at = iotas((KB, width))
    reach = me * C + lax.rem(query_at, C) - key_at

    def rows_of(kb):
        return pl.ds(pl.multiple_of(kb * KB, KB), KB)

    def score(kb, carry):
        kblock = keys[rows_of(kb), :]
        for i in range(parts):
            cols = slice(i * width, (i + 1) * width)
            s = lax.dot_general(kblock, qs[cols, :], NT, preferred_element_type=f32)
            s = jnp.where(reach >= kb * KB, s, NEG_FILL)
            probs[rows_of(kb), cols] = s
            top[:, cols] = jnp.maximum(
                top[:, cols], jnp.max(s.reshape(KB // 8, 8, width), axis=0)
            )
        return carry

    complete(keys, kf_send, kf_recv)
    lax.fori_loop(0, blocks, score, 0)
    peak = jnp.max(top[...], axis=0, keepdims=True)
    top[...] = jnp.broadcast_to(peak, (8, ROWS))

    def take_state(p, carry):
        peer = lax.rem(me + p, N)
        state_copy(peer, peer).wait_recv()
        return carry

    lax.fori_loop(1, N, take_state, 0)

    def slope_copy(peer, source):
        return remote(l_ref.at[peer], lall.at[source], l_send.at[peer], l_recv.at[source], peer)

    def state_of(ref, h):
        return ref[h * QUARTERS : (h + 1) * QUARTERS].reshape(DK, DK).astype(f32)

    gain = gain_ref[...]
    gain_sum = jnp.zeros((1, DK), f32)
    for h in range(HEADS):
        at = slice(h * DK, (h + 1) * DK)
        Q = unit(head_cols(q_ref, h))[0] * DK**-0.5
        K = unit(head_cols(k_ref, h))[0]
        S, W = state_of(srecv, h), w_ref[h]
        cc = cols_s[:, h : h + 1]
        ec = jnp.exp(cc)
        F = fade(cc, rows_s[h : h + 1, :])
        U = u0_ref[h] - d3(W, S, NT)
        Pm = d3(Q, K, NT) * F
        m = ec * d3(Q, S, NT) + d3(Pm, U, NN)
        rr = lax.rsqrt(jnp.mean(m * m, axis=-1, keepdims=True) + 1e-6)
        gate = head_cols(gate_ref, h)
        cot = head_cols(cot_ref, h)
        sig = 1.0 / (1.0 + jnp.exp(-gate))
        silu = gate * sig
        nm = m * rr
        out_ref[:, at] = (nm * gain * silu).astype(bf16)
        dgate_ref[:, at] = (cot * nm * gain * (sig * (1.0 + gate * (1.0 - sig)))).astype(bf16)
        gain_sum = gain_sum + jnp.sum(cot * nm * silu, axis=0, keepdims=True)
        dn = cot * gain * silu
        dO = rr * dn - m * (rr * rr * rr) * jnp.mean(m * dn, axis=-1, keepdims=True)
        dUl = d3(Pm, dO, TN)
        u_ref[h] = U
        do_ref[h] = dO
        dul_ref[h] = dUl
        slope = (d3(ec * dO, Q, TN) - d3(dUl, W, TN)).astype(bf16)
        for q in range(QUARTERS):
            l_ref[h * QUARTERS + q] = slope[q * SROWS : (q + 1) * SROWS, :]

    x_ref[HEADS : 2 * HEADS, :] = jnp.broadcast_to(gain_sum, (HEADS, DK))

    def send_slope(p, carry):
        slope_copy(lax.rem(me + p, N), me).start()
        return carry

    lax.fori_loop(1, N, send_slope, 0)
    lall[me] = l_ref[me]

    pass_on(values, v_send, v_recv, vf_send, vf_recv)
    def weigh(kb, carry):
        vblock = values[rows_of(kb), :]
        for i in range(parts):
            cols = slice(i * width, (i + 1) * width)
            p = jnp.exp(probs[rows_of(kb), cols] - top[0:1, cols])
            probs[rows_of(kb), cols] = p
            low[:, cols] = low[:, cols] + jnp.sum(p.reshape(KB // 8, 8, width), axis=0)
            att[:, cols] = att[:, cols] + lax.dot_general(
                vblock, p.astype(bf16), TN, preferred_element_type=f32
            )
        return carry

    complete(values, vf_send, vf_recv)
    lax.fori_loop(0, blocks, weigh, 0)

    def turn_copy(s, source):
        return remote(tbuf.at[s], trecv.at[source], t_send.at[s], t_recv.at[source], s)

    def back(t, S):
        s = N - 1 - t
        tbuf[s] = S.astype(bf16)

        @pl.when(s != me)
        def _():
            turn_copy(s, me).start()
            slope_copy(s, s).wait_recv()

        return eall[s, 0:1, :] * S + d1(S, mall[s], NT) + lall[s].astype(f32)

    lax.fori_loop(0, N, back, jnp.zeros((SROWS, DK), f32))
    trecv[me] = tbuf[me]
    share = 1.0 / jnp.sum(low[...], axis=0, keepdims=True)
    low[...] = jnp.broadcast_to(share, (8, ROWS))
    for g in range(GROUP):
        cols = slice(g * C, (g + 1) * C)
        at = slice(g * AD, (g + 1) * AD)
        attended = jnp.transpose(att[:, cols] * low[0:1, cols])
        opening = 1.0 / (1.0 + jnp.exp(-ag_ref[:, at].astype(f32)))
        cot = ac_ref[:, at].astype(f32)
        aout_ref[:, at] = (attended * opening).astype(bf16)
        up = (cot * opening).astype(bf16)
        ups[cols, :] = up
        adgate_ref[:, at] = (cot * attended * opening * (1.0 - opening)).astype(bf16)
        center = jnp.sum(jnp.transpose(up.astype(f32) * attended), axis=0, keepdims=True)
        cent[:, cols] = jnp.broadcast_to(center, (8, C))

    def give_copy(c):
        return remote(give.at[c], got.at[c], g_send.at[c], g_recv.at[c], mate)

    def both_copy(c, source):
        return remote(both.at[c], taken.at[source], b_send.at[c], b_recv.at[source], 2 * c + core)

    def grads(kb):
        kblock = keys[rows_of(kb), :]
        vblock = values[rows_of(kb), :]
        dk = jnp.zeros((KB, AD), f32)
        dv = jnp.zeros((KB, AD), f32)
        for i in range(parts):
            cols = slice(i * width, (i + 1) * width)
            p = probs[rows_of(kb), cols] * low[0:1, cols]
            dp = lax.dot_general(vblock, ups[cols, :], NT, preferred_element_type=f32)
            ds = (p * (dp - cent[0:1, cols])).astype(bf16)
            dv = dv + lax.dot_general(p.astype(bf16), ups[cols, :], NN, preferred_element_type=f32)
            dk = dk + lax.dot_general(ds, qs[cols, :], NN, preferred_element_type=f32)
            dqt[:, cols] = dqt[:, cols] + lax.dot_general(
                kblock, ds, TN, preferred_element_type=f32
            )
        block[:, 0:AD] = dk
        block[:, AD : 2 * AD] = dv
        for u in range(KB // (2 * C)):
            c = kb * (KB // (2 * C)) + u
            mine = pl.multiple_of((2 * u + core) * C, C)
            theirs = pl.multiple_of((2 * u + 1 - core) * C, C)
            keep[c] = block[pl.ds(mine, C), :]
            give[c] = block[pl.ds(theirs, C), :].astype(bf16)

            @pl.when(c <= chip)
            def _():
                give_copy(c).start()

    def forward(kb):
        for u in range(KB // (2 * C)):
            c = kb * (KB // (2 * C)) + u

            @pl.when(c <= chip)
            def _():
                give_copy(c).wait_recv()
                both[c] = (keep[c] + got[c].astype(f32)).astype(bf16)

            @pl.when(c < chip)
            def _():
                both_copy(c, chip).start()

    def later(t, carry):
        kb = blocks - 1 - t
        grads(kb)
        forward(kb + 1)
        return carry

    grads(blocks - 1)
    lax.fori_loop(1, blocks, later, 0)
    forward(0)

    def take_turn(p, carry):
        peer = lax.rem(me + p, N)
        turn_copy(peer, peer).wait_recv()
        return carry

    lax.fori_loop(1, N, take_turn, 0)
    lane = lax.broadcasted_iota(jnp.int32, (C, DK), 1)
    sub = lax.broadcasted_iota(jnp.int32, (HEADS, C), 0)
    dbeta = jnp.zeros((C, DK), f32)
    dcol = jnp.zeros((C, DK), f32)
    drow = jnp.zeros((HEADS, C), f32)
    dlast = jnp.zeros((HEADS, C), f32)
    for h in range(HEADS):
        at = slice(h * DK, (h + 1) * DK)
        xq, xk = head_cols(q_ref, h), head_cols(k_ref, h)
        Q0, rq = unit(xq)
        Q = Q0 * DK**-0.5
        K, rk = unit(xk)
        V = head_cols(v_ref, h)
        S, dS = state_of(srecv, h), state_of(trecv, h)
        I, U, dO, dUl = n_ref[h], u_ref[h], do_ref[h], dul_ref[h]
        b, cc = beta_s[:, h : h + 1], cols_s[:, h : h + 1]
        ec = jnp.exp(cc)
        F = fade(cc, rows_s[h : h + 1, :])
        cl = cc[C - 1 : C, :]
        tail = jnp.exp(cl - cc)
        A = d1(K, K, NT)
        QK = d3(Q, K, NT)
        dU = dUl + d3(tail * K, dS, NT)
        QS = ec * d3(Q, S, NT)
        Y = d3(K, S, NT)
        dPF = d3(dO, U, NT) * F
        dQ = ec * d3(dO, S, NN) + d3(dPF, K, NN)
        dKt = tail * d3(U, dS, NN)
        tau = jnp.sum(dKt * K, axis=-1, keepdims=True)
        dcl = jnp.sum(tau, axis=0, keepdims=True) + jnp.exp(cl) * jnp.sum(
            jnp.sum(dS * S, axis=-1, keepdims=True), axis=0, keepdims=True
        )
        dR = d3(I, dU, TN)
        dV = b * dR
        dY = (-ec) * dV
        dLF = jnp.where(r > c, -d3(dR, U, NT), 0.0) * F
        G2 = dLF * A
        db = jnp.sum(dR * (V - ec * Y), axis=-1, keepdims=True) + jnp.sum(
            G2, axis=-1, keepdims=True
        )
        dA = b * dLF
        dK = d3(dPF, Q, TN) + dKt + d3(dY, S, NN) + d3(dA, K, NN) + d3(dA, K, TN)
        G = dPF * QK + b * G2
        dcc = jnp.sum(dO * QS + dY * Y, axis=-1, keepdims=True) - tau + jnp.sum(
            G, axis=-1, keepdims=True
        )
        dbeta = jnp.where(lane == h, db, dbeta)
        dcol = jnp.where(lane == h, dcc, dcol)
        drow = jnp.where(sub == h, -jnp.sum(G, axis=0, keepdims=True), drow)
        dlast = jnp.where(sub == h, dcl, dlast)
        dq_ref[:, at] = (
            DK**-0.5 * (rq * dQ - xq * (rq * rq * rq) * jnp.sum(xq * dQ, axis=-1, keepdims=True))
        ).astype(bf16)
        dk_ref[:, at] = (
            rk * dK - xk * (rk * rk * rk) * jnp.sum(xk * dK, axis=-1, keepdims=True)
        ).astype(bf16)
        dv_ref[:, at] = dV.astype(bf16)
    since = jnp.where(r >= c, 1.0, 0.0)
    dg = dfull(dcol, since, TN)[:HEADS] + dfull(drow, since, NN) + dlast
    dbeta = dfull(dbeta, jnp.where(r == c, 1.0, 0.0), TN)[:HEADS]
    dbl_ref[...] = dbeta * beta_rows * (1.0 - beta_rows)
    ddi_ref[...] = dg * rate / (1.0 + jnp.exp(-di_ref[...]))
    x_ref[0:HEADS, :] = jnp.zeros((HEADS, DK), f32)
    x_ref[0:HEADS, 0:HEADS] = dfull(jnp.ones((HEADS, C), f32), dg * decay, NT)

    def pair_copy():
        return remote(x_ref, pairs, p_send, p_recv, mate)

    def every_copy(p, source):
        peer = lax.rem(chip + p, CHIPS) * 2 + core
        return remote(part, every.at[source], e_send.at[p], e_recv.at[source], peer)

    def aside_copy(i):
        return remote(total, others.at[i], a_send.at[i], a_recv.at[i], aside(i))

    pair_copy().start()
    for g in range(GROUP):
        cols = slice(g * C, (g + 1) * C)
        adq_ref[:, g * AD : (g + 1) * AD] = (jnp.transpose(dqt[:, cols]) * scale).astype(bf16)

    pair_copy().wait()
    part[...] = x_ref[...] + pairs[...]

    def send_part(p, carry):
        every_copy(p, chip).start()
        return carry

    lax.fori_loop(1, CHIPS, send_part, 0)
    every[chip] = part[...]
    def take_part(p, carry):
        source = lax.rem(chip + p, CHIPS)
        every_copy(p, chip).wait_send()
        every_copy(p, source).wait_recv()
        return carry

    lax.fori_loop(1, CHIPS, take_part, 0)
    total[...] = jnp.sum(every[...], axis=0)
    for i in range(3):
        aside_copy(i).start()


    keep[chip] = keep[chip] + got[chip].astype(f32)

    def collect(t, carry):
        source = chip + 1 + t
        both_copy(source, source).wait_recv()
        keep[chip] = keep[chip] + taken[source].astype(f32)
        return carry

    def sent(c, carry):
        give_copy(c).wait_send()

        @pl.when(c < chip)
        def _():
            both_copy(c, chip).wait_send()

        return carry

    lax.fori_loop(0, CHIPS - 1 - chip, collect, 0)
    adk_ref[...] = keep[chip, :, 0:AD].astype(bf16)
    adv_ref[...] = keep[chip, :, AD : 2 * AD].astype(bf16)
    lax.fori_loop(0, chip + 1, sent, 0)
    for i in range(3):
        aside_copy(i).wait()
    same = slice(0, HEADS)
    gain = slice(HEADS, 2 * HEADS)
    sums_ref[same, :] = total[same, :] + others[0, same, :]
    sums_ref[gain, :] = (total[gain, :] + others[0, gain, :]) + (
        others[1, gain, :] + others[2, gain, :]
    )

    def drain(p, carry):
        peer = lax.rem(me + p, N)
        offset_copy(peer, me).wait_send()
        state_copy(peer, me).wait_send()
        slope_copy(peer, me).wait_send()
        turn_copy(peer, me).wait_send()
        return carry

    def drain_map(p, carry):
        map_copy(lax.rem(chip + p, CHIPS) * 2 + core, me).wait_send()
        return carry

    def drain_pass(cc, carry):
        map_pass(2 * cc + core).wait_send()
        return carry

    def drain_wide(to, carry):
        wide_copy(keys, k_send, k_recv, to, chip).wait_send()
        wide_copy(values, v_send, v_recv, to, chip).wait_send()
        return carry

    def drain_wide_pass(source, carry):
        wide_pass(keys, kf_send, kf_recv, core, source).wait_send()
        wide_pass(values, vf_send, vf_recv, core, source).wait_send()
        return carry

    lax.fori_loop(1, N, drain, 0)
    lax.fori_loop(1, CHIPS, drain_map, 0)
    lax.fori_loop(0, CHIPS, drain_pass, 0)
    lax.fori_loop(chip + 1, CHIPS, drain_wide, 0)
    lax.fori_loop(0, chip + 1, drain_wide_pass, 0)


def place_kernel(count, sums_ref, *refs):
    ins, outs = refs[:count], refs[count : 2 * count]
    log_ref, gain_ref, sems = refs[2 * count :]
    copies = [pltpu.make_async_copy(a, b, sems.at[i]) for i, (a, b) in enumerate(zip(ins, outs))]
    for copy in copies:
        copy.start()
    log_ref[...] = sums_ref[0:1, 0:HEADS]
    gain_ref[...] = sums_ref[HEADS : HEADS + 1, :]
    for copy in copies:
        copy.wait()


VM = pl.BlockSpec(memory_space=pltpu.VMEM)
SM = pl.BlockSpec(memory_space=pltpu.SMEM)
ANY = pl.BlockSpec(memory_space=pl.ANY)


def per_device(
    delta_query, delta_key, delta_value, beta_logit, decay_input, decay_log, norm_gain,
    output_gate, delta_cotangent, attn_query, attn_key, attn_value, attn_gate, attn_cotangent,
):
    wide, flat, own = (C, HEADS * DK), (C, GROUP * AD), (C, AD)
    rows, pair = (HEADS, C), (2 * HEADS, DK)
    square, states = (HEADS, DK, DK), (N, SROWS, DK)
    loaded = (N, SROWS + KEEP, DK)
    blocks = (CHIPS, C, 2 * AD)
    args = (
        delta_query[0], delta_key[0], delta_value[0], beta_logit[0].T, decay_input[0].T, decay_log,
        norm_gain[None], output_gate[0], delta_cotangent[0],
        attn_query[0], attn_key[0], attn_value[0], attn_gate[0], attn_cotangent[0],
    )

    def vm(shape, dtype=f32):
        return pltpu.VMEM(shape, dtype)

    def dma(count):
        return pltpu.SemaphoreType.DMA((count,))

    one = pltpu.SemaphoreType.DMA
    shapes = [(wide, bf16)] * 4 + [(rows, f32)] * 2 + [(wide, bf16)]
    shapes += [(flat, bf16)] * 2 + [(own, bf16)] * 2 + [(flat, bf16), (pair, f32)]
    shapes = [jax.ShapeDtypeStruct(s, d) for s, d in shapes]
    results = pl.pallas_call(
        whole_kernel,
        out_shape=tuple(shapes),
        in_specs=[SM if x.ndim == 1 else VM for x in args],
        out_specs=tuple(VM for _ in shapes),
        scratch_shapes=[vm((C, HEADS)), vm((C, HEADS)), vm(rows)]
        + [vm(square)] * 6
        + [vm(square, bf16), vm(loaded, bf16), vm((N, DK, DK), bf16), vm(loaded, bf16)]
        + [vm((N, 8, DK))]
        + [vm(states, bf16)] * 6
        + [vm((LENGTH, AD), bf16)] * 2
        + [vm((ROWS, AD), bf16)] * 2
        + [vm((LENGTH, ROWS)), vm((AD, ROWS)), vm((AD, ROWS))]
        + [vm((8, ROWS))] * 3
        + [vm((KB, 2 * AD)), vm(blocks)]
        + [vm(blocks, bf16)] * 4
        + [vm(pair), vm(pair), vm(pair), vm((CHIPS,) + pair), vm(pair), vm((3,) + pair)]
        + [dma(N)] * 12
        + [dma(CHIPS)] * 12
        + [one, one]
        + [dma(CHIPS)] * 2
        + [dma(3)] * 2,
        compiler_params=pltpu.CompilerParams(
            vmem_limit_bytes=VMEM_BIG, collective_id=1, has_side_effects=True
        ),
    )(*args)
    results, sums = results[:-1], results[-1]
    count = len(results)
    *placed, log_grad, gain_grad = pl.pallas_call(
        functools.partial(place_kernel, count),
        out_shape=tuple(shapes[:-1])
        + (jax.ShapeDtypeStruct((1, HEADS), f32), jax.ShapeDtypeStruct((1, DK), f32)),
        in_specs=[VM] + [ANY] * count,
        out_specs=(VM,) * (count + 2),
        scratch_shapes=[dma(count)],
        compiler_params=pltpu.CompilerParams(vmem_limit_bytes=VMEM_BIG),
    )(sums, *results)
    out, dq, dk, dv, dbl, ddi, dgate, aout, adq, adk, adv, adgate = placed
    return (
        out[None], dq[None], dk[None], dv[None], dbl.T[None], ddi.T[None], log_grad[0], gain_grad[0],
        dgate[None], aout[None], adq[None], adk[None], adv[None], adgate[None],
    )


def solution(mesh):
    split3 = P("section", "ctx", "head")
    in_specs = (split3,) * 5 + (P("head"), P()) + (split3,) * 7
    out_specs = (split3,) * 6 + (P("head"), P()) + (split3,) * 6
    return jax.shard_map(
        per_device, mesh=mesh, in_specs=in_specs, out_specs=out_specs, check_vma=False
    )
```

```python
import functools

import jax
import jax.numpy as jnp
from jax import lax
from jax.experimental import pallas as pl
from jax.experimental.pallas import tpu as pltpu
from jax.sharding import PartitionSpec as P

f32, bf16 = jnp.float32, jnp.bfloat16
MESH = pl.DeviceIdType.MESH
HIGHEST = lax.Precision.HIGHEST
NEG_FILL = -1e30
N = 32
C = 128
DK = 128
AD = 256
HEADS = 8
GROUP = 8
ROWS = GROUP * C
KB = 512
LENGTH = N * C
NKB = LENGTH // KB
QUARTERS = N // HEADS
SROWS = DK // QUARTERS
KEEP = 16
CHIPS = N // 2
VMEM_BIG = 60 * 1024 * 1024

NT = (((1,), (1,)), ((), ()))
NN = (((1,), (0,)), ((), ()))
TN = (((0,), (0,)), ((), ()))


def d1(a, b, dims):
    return lax.dot_general(a.astype(bf16), b.astype(bf16), dims, preferred_element_type=f32)


def split(a):
    hi = a.astype(bf16)
    return hi, (a - hi.astype(f32)).astype(bf16)


def d3(a, b, dims):
    ah, al = split(a)
    bh, bl = split(b)

    def dot(x, y):
        return lax.dot_general(x, y, dims, preferred_element_type=f32)

    return dot(ah, bh) + (dot(ah, bl) + dot(al, bh))


def dfull(a, b, dims):
    return lax.dot_general(a, b, dims, precision=HIGHEST, preferred_element_type=f32)


def iotas(shape=(C, C)):
    return (
        lax.broadcasted_iota(jnp.int32, shape, 0),
        lax.broadcasted_iota(jnp.int32, shape, 1),
    )


def unit(x):
    r = lax.rsqrt(jnp.sum(x * x, axis=-1, keepdims=True) + 1e-6)
    return x * r, r


def gates_of(bl_ref, di_ref, dl_ref):
    beta = 1.0 / (1.0 + jnp.exp(-bl_ref[...]))
    a = di_ref[...]
    head = lax.broadcasted_iota(jnp.int32, a.shape, 0)
    logs = jnp.zeros(a.shape, f32)
    for h in range(HEADS):
        logs = jnp.where(head == h, dl_ref[h], logs)
    rate = -jnp.exp(logs)
    soft = jnp.maximum(a, 0.0) + jnp.log1p(jnp.exp(-jnp.abs(a)))
    g = jnp.maximum(rate * soft, -104.0)
    r, c = iotas()
    beta_cols = dfull(jnp.where(r == c, 1.0, 0.0), beta, NT)
    cols = dfull(jnp.where(r >= c, 1.0, 0.0), g, NT)
    rows = dfull(g, jnp.where(r <= c, 1.0, 0.0), NN)
    return beta, g, rate, beta_cols, cols, rows


def fade(cc, cr):
    r, c = iotas()
    return jnp.where(r >= c, jnp.exp(jnp.where(r >= c, cc - cr, 0.0)), 0.0)


def head_cols(ref, h):
    return ref[:, h * DK : (h + 1) * DK].astype(f32)


def peers_of(me):
    core = lax.rem(me, 2)
    return me // 2, core, me + 1 - 2 * core


def remote(src, dst, send, recv, peer):
    if not isinstance(peer, dict):
        peer = {"ctx": peer}
    return pltpu.make_async_remote_copy(
        src_ref=src, dst_ref=dst, send_sem=send, recv_sem=recv, device_id=peer, device_id_type=MESH
    )


def whole_kernel(
    q_ref, k_ref, v_ref, bl_ref, di_ref, dl_ref, gain_ref, gate_ref, cot_ref,
    aq_hbm, ak_ref, av_ref, ag_hbm, ac_hbm,
    out_hbm, dq_hbm, dk_hbm, dv_hbm, dbl_ref, ddi_ref, dgate_hbm,
    aout_hbm, adq_hbm, adk_ref, adv_ref, adgate_hbm, sums_ref,
    aq_ref, ag_ref, ac_ref, out_ref, dq_ref, dk_ref, dv_ref, dgate_ref, aout_ref, adq_ref, adgate_ref,
    load, store,
    beta_s, cols_s, rows_s, n_ref, w_ref, u0_ref, u_ref, do_ref, dul_ref,
    m_ref, o_ref, mall, oall, eall, sbuf, srecv, l_ref, lall, tbuf, trecv,
    keys, values,
    qs, ups, probs, att, dqt, top, low, cent, block, keep, give, got, both, taken,
    x_ref, pairs, part, every, total, others,
    m_send, m_recv, f_send, f_recv, o_send, o_recv, s_send, s_recv, l_send, l_recv, t_send, t_recv,
    k_send, k_recv, kf_send, kf_recv, v_send, v_recv, vf_send, vf_recv,
    g_send, g_recv, b_send, b_recv, p_send, p_recv, e_send, e_recv, a_send, a_recv,
):
    me, head, section = (lax.axis_index(a) for a in ("ctx", "head", "section"))
    chip, core, mate = peers_of(me)
    barrier = pltpu.get_barrier_semaphore()
    ahead = ((aq_hbm, aq_ref), (ag_hbm, ag_ref), (ac_hbm, ac_ref))
    loads = [pltpu.make_async_copy(a, b, load.at[i]) for i, (a, b) in enumerate(ahead)]
    for copy in loads:
        copy.start()
    turns = ((0, 1), (1, 0), (1, 1))

    def aside(i):
        dh, ds = turns[i]
        return {"head": lax.rem(head + dh, 2), "section": lax.rem(section + ds, 2)}

    def hello(p, carry):
        pl.semaphore_signal(
            barrier, inc=1, device_id={"ctx": lax.rem(me + p, N)}, device_id_type=MESH
        )
        return carry

    lax.fori_loop(1, N, hello, 0)
    for i in range(3):
        pl.semaphore_signal(barrier, inc=1, device_id=aside(i), device_id_type=MESH)

    r, c = iotas()
    beta_rows, decay, rate, beta, cols, rows = gates_of(bl_ref, di_ref, dl_ref)
    beta_s[...] = beta
    cols_s[...] = cols
    rows_s[...] = rows

    def own_rows(device):
        return pl.ds(pl.multiple_of(device * C, C), C)

    def wide_copy(ref, send, recv, to, source):
        at = own_rows(2 * source + core)
        return remote(ref.at[at, :], ref.at[at, :], send.at[to], recv.at[source], 2 * to + core)

    def wide_pass(ref, send, recv, which, source):
        at = own_rows(2 * source + which)
        return remote(ref.at[at, :], ref.at[at, :], send.at[source], recv.at[source], mate)

    def spread(own, ref, send, recv):
        ref[own_rows(me), :] = own[...]

        @pl.when(lax.rem(chip, 2) == 0)
        def _():
            ref[pl.ds(pl.multiple_of((chip + 1) * 2 * C, C), 2 * C), :] = jnp.zeros((2 * C, AD), bf16)

        def go(to, carry):
            wide_copy(ref, send, recv, to, chip).start()
            return carry

        lax.fori_loop(chip + 1, CHIPS, go, 0)

    def pass_on(ref, send, recv, pass_send, pass_recv):
        wide_pass(ref, pass_send, pass_recv, core, chip).start()

        def go(t, carry):
            source = chip - t
            wide_copy(ref, send, recv, source, source).wait_recv()
            wide_pass(ref, pass_send, pass_recv, core, source).start()
            return carry

        lax.fori_loop(1, chip + 1, go, 0)

    def complete(ref, pass_send, pass_recv):
        def go(source, carry):
            wide_pass(ref, pass_send, pass_recv, 1 - core, source).wait_recv()
            return carry

        lax.fori_loop(0, chip + 1, go, 0)

    pl.semaphore_wait(barrier, N + 2)
    spread(ak_ref, keys, k_send, k_recv)

    def chunk(heads):
        ks = [unit(head_cols(k_ref, h))[0] for h in heads]
        lows = []
        for h, K in zip(heads, ks):
            F = fade(cols[:, h : h + 1], rows[h : h + 1, :])
            lows.append(jnp.where(r > c, beta[:, h : h + 1] * F * d1(K, K, NT), 0.0))
        inv = [
            jnp.where(r == c, 1.0, 0.0) - jnp.where(r // 2 == c // 2, L, 0.0) for L in lows
        ]
        k = 2
        while k < C:
            part_k = (r // (2 * k) == c // (2 * k)) & (r // k != c // k)
            mid = [d1(I, jnp.where(part_k, L, 0.0), NN) for I, L in zip(inv, lows)]
            inv = [I - d1(T, I, NN) for I, T in zip(inv, mid)]
            k *= 2
        for h, K, I in zip(heads, ks, inv):
            b, cc = beta[:, h : h + 1], cols[:, h : h + 1]
            V = head_cols(v_ref, h)
            W = d3(I, (b * jnp.exp(cc)) * K, NN)
            U0 = d3(I, b * V, NN)
            cl = cc[C - 1 : C, :]
            Kt = jnp.exp(cl - cc) * K
            n_ref[h] = I
            w_ref[h] = W
            u0_ref[h] = U0
            m_ref[h] = (-d3(W, Kt, TN)).astype(bf16)
            off = d3(U0, Kt, TN).astype(bf16)
            stay = jnp.broadcast_to(jnp.exp(cl), (KEEP, DK))
            high = stay.astype(bf16)
            mid = (stay - high.astype(f32)).astype(bf16)
            last = stay - high.astype(f32) - mid.astype(f32)
            row = lax.broadcasted_iota(jnp.int32, (KEEP, DK), 0)
            terms = jnp.where(row == 0, high.astype(f32), jnp.where(row == 1, mid.astype(f32), last))
            for q in range(QUARTERS):
                o_ref[h * QUARTERS + q, 0:SROWS, :] = off[q * SROWS : (q + 1) * SROWS, :]
                o_ref[h * QUARTERS + q, SROWS : SROWS + KEEP, :] = terms.astype(bf16)

    def map_copy(peer, source):
        return remote(
            m_ref.at[peer // QUARTERS], mall.at[source], m_send.at[peer // 2], m_recv.at[source], peer
        )

    def offset_copy(peer, source):
        return remote(o_ref.at[peer], oall.at[source], o_send.at[peer], o_recv.at[source], peer)

    half = CHIPS // 2
    for first in (0, 1):
        chunk(range(first * HEADS // 2, (first + 1) * HEADS // 2))
        def send_map(t, carry):
            to = first * half + lax.rem(chip + t, half)

            @pl.when(to != chip)
            def _():
                map_copy(2 * to + core, me).start()

            return carry

        def send_offset(t, carry):
            to = first * N // 2 + lax.rem(me + t, N // 2)

            @pl.when(to != me)
            def _():
                offset_copy(to, me).start()

            return carry

        lax.fori_loop(0, half, send_map, 0)
        lax.fori_loop(0, N // 2, send_offset, 0)
    mall[me] = m_ref[me // QUARTERS]
    oall[me] = o_ref[me]


    def map_pass(source):
        return remote(mall.at[source], mall.at[source], f_send.at[source], f_recv.at[source], mate)

    def state_copy(s, source):
        return remote(sbuf.at[s], srecv.at[source], s_send.at[s], s_recv.at[source], s)

    def arrive(cc):
        source = 2 * cc + core

        @pl.when(source != me)
        def _():
            map_copy(source, source).wait_recv()

        map_pass(source).start()

    def advance(s, S):
        @pl.when(s != me)
        def _():
            offset_copy(s, s).wait_recv()

        sbuf[s] = S.astype(bf16)

        @pl.when(s != me)
        def _():
            state_copy(s, me).start()

        terms = oall[s, SROWS : SROWS + KEEP, :].astype(f32)
        stay = terms[0:1] + (terms[1:2] + terms[2:3])
        eall[s] = jnp.broadcast_to(stay, (8, DK))
        return stay * S + d1(S, mall[s], NN) + oall[s, 0:SROWS, :].astype(f32)

    def pair(cc, S):
        map_pass(2 * cc + 1 - core).wait_recv()
        return advance(2 * cc + 1, advance(2 * cc, S))

    def forth(cc, S):
        arrive(cc)
        return pair(cc - 1, S)

    arrive(0)
    S_end = lax.fori_loop(1, CHIPS, forth, jnp.zeros((SROWS, DK), f32))
    pair(CHIPS - 1, S_end)
    srecv[me] = sbuf[me]

    spread(av_ref, values, v_send, v_recv)
    pass_on(keys, k_send, k_recv, kf_send, kf_recv)

    for copy in loads:
        copy.wait()
    blocks = me // (KB // C) + 1
    scale = AD**-0.5
    width = 256
    parts = ROWS // width
    for g in range(GROUP):
        qs[g * C : (g + 1) * C, :] = (
            aq_ref[:, g * AD : (g + 1) * AD].astype(f32) * scale
        ).astype(bf16)
    top[...] = jnp.full((8, ROWS), NEG_FILL, f32)
    low[...] = jnp.zeros((8, ROWS), f32)
    att[...] = jnp.zeros((AD, ROWS), f32)
    dqt[...] = jnp.zeros((AD, ROWS), f32)
    key_at, query_at = iotas((KB, width))
    reach = me * C + lax.rem(query_at, C) - key_at

    def rows_of(kb):
        return pl.ds(pl.multiple_of(kb * KB, KB), KB)

    def score(kb, carry):
        kblock = keys[rows_of(kb), :]
        for i in range(parts):
            cols = slice(i * width, (i + 1) * width)
            s = lax.dot_general(kblock, qs[cols, :], NT, preferred_element_type=f32)
            s = jnp.where(reach >= kb * KB, s, NEG_FILL)
            probs[rows_of(kb), cols] = s
            top[:, cols] = jnp.maximum(
                top[:, cols], jnp.max(s.reshape(KB // 8, 8, width), axis=0)
            )
        return carry

    complete(keys, kf_send, kf_recv)
    lax.fori_loop(0, blocks, score, 0)
    peak = jnp.max(top[...], axis=0, keepdims=True)
    top[...] = jnp.broadcast_to(peak, (8, ROWS))

    def take_state(p, carry):
        peer = lax.rem(me + p, N)
        state_copy(peer, peer).wait_recv()
        return carry

    lax.fori_loop(1, N, take_state, 0)

    def slope_copy(peer, source):
        return remote(l_ref.at[peer], lall.at[source], l_send.at[peer], l_recv.at[source], peer)

    def state_of(ref, h):
        return ref[h * QUARTERS : (h + 1) * QUARTERS].reshape(DK, DK).astype(f32)

    gain = gain_ref[...]
    gain_sum = jnp.zeros((1, DK), f32)
    for h in range(HEADS):
        at = slice(h * DK, (h + 1) * DK)
        Q = unit(head_cols(q_ref, h))[0] * DK**-0.5
        K = unit(head_cols(k_ref, h))[0]
        S, W = state_of(srecv, h), w_ref[h]
        cc = cols_s[:, h : h + 1]
        ec = jnp.exp(cc)
        F = fade(cc, rows_s[h : h + 1, :])
        U = u0_ref[h] - d3(W, S, NT)
        Pm = d3(Q, K, NT) * F
        m = ec * d3(Q, S, NT) + d3(Pm, U, NN)
        rr = lax.rsqrt(jnp.mean(m * m, axis=-1, keepdims=True) + 1e-6)
        gate = head_cols(gate_ref, h)
        cot = head_cols(cot_ref, h)
        sig = 1.0 / (1.0 + jnp.exp(-gate))
        silu = gate * sig
        nm = m * rr
        out_ref[:, at] = (nm * gain * silu).astype(bf16)
        dgate_ref[:, at] = (cot * nm * gain * (sig * (1.0 + gate * (1.0 - sig)))).astype(bf16)
        gain_sum = gain_sum + jnp.sum(cot * nm * silu, axis=0, keepdims=True)
        dn = cot * gain * silu
        dO = rr * dn - m * (rr * rr * rr) * jnp.mean(m * dn, axis=-1, keepdims=True)
        dUl = d3(Pm, dO, TN)
        u_ref[h] = U
        do_ref[h] = dO
        dul_ref[h] = dUl
        slope = (d3(ec * dO, Q, TN) - d3(dUl, W, TN)).astype(bf16)
        for q in range(QUARTERS):
            l_ref[h * QUARTERS + q] = slope[q * SROWS : (q + 1) * SROWS, :]

    x_ref[HEADS : 2 * HEADS, :] = jnp.broadcast_to(gain_sum, (HEADS, DK))

    def send_slope(p, carry):
        slope_copy(lax.rem(me + p, N), me).start()
        return carry

    lax.fori_loop(1, N, send_slope, 0)
    lall[me] = l_ref[me]

    pass_on(values, v_send, v_recv, vf_send, vf_recv)
    def weigh(kb, carry):
        vblock = values[rows_of(kb), :]
        for i in range(parts):
            cols = slice(i * width, (i + 1) * width)
            p = jnp.exp(probs[rows_of(kb), cols] - top[0:1, cols])
            probs[rows_of(kb), cols] = p
            low[:, cols] = low[:, cols] + jnp.sum(p.reshape(KB // 8, 8, width), axis=0)
            att[:, cols] = att[:, cols] + lax.dot_general(
                vblock, p.astype(bf16), TN, preferred_element_type=f32
            )
        return carry

    complete(values, vf_send, vf_recv)
    lax.fori_loop(0, blocks, weigh, 0)

    def turn_copy(s, source):
        return remote(tbuf.at[s], trecv.at[source], t_send.at[s], t_recv.at[source], s)

    def back(t, S):
        s = N - 1 - t
        tbuf[s] = S.astype(bf16)

        @pl.when(s != me)
        def _():
            turn_copy(s, me).start()
            slope_copy(s, s).wait_recv()

        return eall[s, 0:1, :] * S + d1(S, mall[s], NT) + lall[s].astype(f32)

    lax.fori_loop(0, N, back, jnp.zeros((SROWS, DK), f32))
    trecv[me] = tbuf[me]
    share = 1.0 / jnp.sum(low[...], axis=0, keepdims=True)
    low[...] = jnp.broadcast_to(share, (8, ROWS))
    for g in range(GROUP):
        cols = slice(g * C, (g + 1) * C)
        at = slice(g * AD, (g + 1) * AD)
        attended = jnp.transpose(att[:, cols] * low[0:1, cols])
        opening = 1.0 / (1.0 + jnp.exp(-ag_ref[:, at].astype(f32)))
        cot = ac_ref[:, at].astype(f32)
        aout_ref[:, at] = (attended * opening).astype(bf16)
        up = (cot * opening).astype(bf16)
        ups[cols, :] = up
        adgate_ref[:, at] = (cot * attended * opening * (1.0 - opening)).astype(bf16)
        center = jnp.sum(jnp.transpose(up.astype(f32) * attended), axis=0, keepdims=True)
        cent[:, cols] = jnp.broadcast_to(center, (8, C))

    def give_copy(c):
        return remote(give.at[c], got.at[c], g_send.at[c], g_recv.at[c], mate)

    def both_copy(c, source):
        return remote(both.at[c], taken.at[source], b_send.at[c], b_recv.at[source], 2 * c + core)

    def grads(kb):
        kblock = keys[rows_of(kb), :]
        vblock = values[rows_of(kb), :]
        dk = jnp.zeros((KB, AD), f32)
        dv = jnp.zeros((KB, AD), f32)
        for i in range(parts):
            cols = slice(i * width, (i + 1) * width)
            p = probs[rows_of(kb), cols] * low[0:1, cols]
            dp = lax.dot_general(vblock, ups[cols, :], NT, preferred_element_type=f32)
            ds = (p * (dp - cent[0:1, cols])).astype(bf16)
            dv = dv + lax.dot_general(p.astype(bf16), ups[cols, :], NN, preferred_element_type=f32)
            dk = dk + lax.dot_general(ds, qs[cols, :], NN, preferred_element_type=f32)
            dqt[:, cols] = dqt[:, cols] + lax.dot_general(
                kblock, ds, TN, preferred_element_type=f32
            )
        block[:, 0:AD] = dk
        block[:, AD : 2 * AD] = dv
        for u in range(KB // (2 * C)):
            c = kb * (KB // (2 * C)) + u
            mine = pl.multiple_of((2 * u + core) * C, C)
            theirs = pl.multiple_of((2 * u + 1 - core) * C, C)
            keep[c] = block[pl.ds(mine, C), :]
            give[c] = block[pl.ds(theirs, C), :].astype(bf16)

            @pl.when(c <= chip)
            def _():
                give_copy(c).start()

    def forward(kb):
        for u in range(KB // (2 * C)):
            c = kb * (KB // (2 * C)) + u

            @pl.when(c <= chip)
            def _():
                give_copy(c).wait_recv()
                both[c] = (keep[c] + got[c].astype(f32)).astype(bf16)

            @pl.when(c < chip)
            def _():
                both_copy(c, chip).start()

    def later(t, carry):
        kb = blocks - 1 - t
        grads(kb)
        forward(kb + 1)
        return carry

    grads(blocks - 1)
    lax.fori_loop(1, blocks, later, 0)
    forward(0)

    def take_turn(p, carry):
        peer = lax.rem(me + p, N)
        turn_copy(peer, peer).wait_recv()
        return carry

    lax.fori_loop(1, N, take_turn, 0)
    lane = lax.broadcasted_iota(jnp.int32, (C, DK), 1)
    sub = lax.broadcasted_iota(jnp.int32, (HEADS, C), 0)
    dbeta = jnp.zeros((C, DK), f32)
    dcol = jnp.zeros((C, DK), f32)
    drow = jnp.zeros((HEADS, C), f32)
    dlast = jnp.zeros((HEADS, C), f32)
    for h in range(HEADS):
        at = slice(h * DK, (h + 1) * DK)
        xq, xk = head_cols(q_ref, h), head_cols(k_ref, h)
        Q0, rq = unit(xq)
        Q = Q0 * DK**-0.5
        K, rk = unit(xk)
        V = head_cols(v_ref, h)
        S, dS = state_of(srecv, h), state_of(trecv, h)
        I, U, dO, dUl = n_ref[h], u_ref[h], do_ref[h], dul_ref[h]
        b, cc = beta_s[:, h : h + 1], cols_s[:, h : h + 1]
        ec = jnp.exp(cc)
        F = fade(cc, rows_s[h : h + 1, :])
        cl = cc[C - 1 : C, :]
        tail = jnp.exp(cl - cc)
        A = d1(K, K, NT)
        QK = d3(Q, K, NT)
        dU = dUl + d3(tail * K, dS, NT)
        QS = ec * d3(Q, S, NT)
        Y = d3(K, S, NT)
        dPF = d3(dO, U, NT) * F
        dQ = ec * d3(dO, S, NN) + d3(dPF, K, NN)
        dKt = tail * d3(U, dS, NN)
        tau = jnp.sum(dKt * K, axis=-1, keepdims=True)
        dcl = jnp.sum(tau, axis=0, keepdims=True) + jnp.exp(cl) * jnp.sum(
            jnp.sum(dS * S, axis=-1, keepdims=True), axis=0, keepdims=True
        )
        dR = d3(I, dU, TN)
        dV = b * dR
        dY = (-ec) * dV
        dLF = jnp.where(r > c, -d3(dR, U, NT), 0.0) * F
        G2 = dLF * A
        db = jnp.sum(dR * (V - ec * Y), axis=-1, keepdims=True) + jnp.sum(
            G2, axis=-1, keepdims=True
        )
        dA = b * dLF
        dK = d3(dPF, Q, TN) + dKt + d3(dY, S, NN) + d3(dA, K, NN) + d3(dA, K, TN)
        G = dPF * QK + b * G2
        dcc = jnp.sum(dO * QS + dY * Y, axis=-1, keepdims=True) - tau + jnp.sum(
            G, axis=-1, keepdims=True
        )
        dbeta = jnp.where(lane == h, db, dbeta)
        dcol = jnp.where(lane == h, dcc, dcol)
        drow = jnp.where(sub == h, -jnp.sum(G, axis=0, keepdims=True), drow)
        dlast = jnp.where(sub == h, dcl, dlast)
        dq_ref[:, at] = (
            DK**-0.5 * (rq * dQ - xq * (rq * rq * rq) * jnp.sum(xq * dQ, axis=-1, keepdims=True))
        ).astype(bf16)
        dk_ref[:, at] = (
            rk * dK - xk * (rk * rk * rk) * jnp.sum(xk * dK, axis=-1, keepdims=True)
        ).astype(bf16)
        dv_ref[:, at] = dV.astype(bf16)
    since = jnp.where(r >= c, 1.0, 0.0)
    dg = dfull(dcol, since, TN)[:HEADS] + dfull(drow, since, NN) + dlast
    dbeta = dfull(dbeta, jnp.where(r == c, 1.0, 0.0), TN)[:HEADS]
    dbl_ref[...] = dbeta * beta_rows * (1.0 - beta_rows)
    ddi_ref[...] = dg * rate / (1.0 + jnp.exp(-di_ref[...]))
    x_ref[0:HEADS, :] = jnp.zeros((HEADS, DK), f32)
    x_ref[0:HEADS, 0:HEADS] = dfull(jnp.ones((HEADS, C), f32), dg * decay, NT)

    def pair_copy():
        return remote(x_ref, pairs, p_send, p_recv, mate)

    def every_copy(p, source):
        peer = lax.rem(chip + p, CHIPS) * 2 + core
        return remote(part, every.at[source], e_send.at[p], e_recv.at[source], peer)

    def aside_copy(i):
        return remote(total, others.at[i], a_send.at[i], a_recv.at[i], aside(i))

    pair_copy().start()
    for g in range(GROUP):
        cols = slice(g * C, (g + 1) * C)
        adq_ref[:, g * AD : (g + 1) * AD] = (jnp.transpose(dqt[:, cols]) * scale).astype(bf16)

    behind = (
        (out_ref, out_hbm), (dq_ref, dq_hbm), (dk_ref, dk_hbm), (dv_ref, dv_hbm),
        (dgate_ref, dgate_hbm), (aout_ref, aout_hbm), (adq_ref, adq_hbm), (adgate_ref, adgate_hbm),
    )
    stores = [pltpu.make_async_copy(a, b, store.at[i]) for i, (a, b) in enumerate(behind)]
    for copy in stores:
        copy.start()
    pair_copy().wait()
    part[...] = x_ref[...] + pairs[...]

    def send_part(p, carry):
        every_copy(p, chip).start()
        return carry

    lax.fori_loop(1, CHIPS, send_part, 0)
    every[chip] = part[...]
    def take_part(p, carry):
        source = lax.rem(chip + p, CHIPS)
        every_copy(p, chip).wait_send()
        every_copy(p, source).wait_recv()
        return carry

    lax.fori_loop(1, CHIPS, take_part, 0)
    total[...] = jnp.sum(every[...], axis=0)
    for i in range(3):
        aside_copy(i).start()


    keep[chip] = keep[chip] + got[chip].astype(f32)

    def collect(t, carry):
        source = chip + 1 + t
        both_copy(source, source).wait_recv()
        keep[chip] = keep[chip] + taken[source].astype(f32)
        return carry

    def sent(c, carry):
        give_copy(c).wait_send()

        @pl.when(c < chip)
        def _():
            both_copy(c, chip).wait_send()

        return carry

    lax.fori_loop(0, CHIPS - 1 - chip, collect, 0)
    adk_ref[...] = keep[chip, :, 0:AD].astype(bf16)
    adv_ref[...] = keep[chip, :, AD : 2 * AD].astype(bf16)
    lax.fori_loop(0, chip + 1, sent, 0)
    for i in range(3):
        aside_copy(i).wait()
    same = slice(0, HEADS)
    gain = slice(HEADS, 2 * HEADS)
    sums_ref[same, :] = total[same, :] + others[0, same, :]
    sums_ref[gain, :] = (total[gain, :] + others[0, gain, :]) + (
        others[1, gain, :] + others[2, gain, :]
    )

    def drain(p, carry):
        peer = lax.rem(me + p, N)
        offset_copy(peer, me).wait_send()
        state_copy(peer, me).wait_send()
        slope_copy(peer, me).wait_send()
        turn_copy(peer, me).wait_send()
        return carry

    def drain_map(p, carry):
        map_copy(lax.rem(chip + p, CHIPS) * 2 + core, me).wait_send()
        return carry

    def drain_pass(cc, carry):
        map_pass(2 * cc + core).wait_send()
        return carry

    def drain_wide(to, carry):
        wide_copy(keys, k_send, k_recv, to, chip).wait_send()
        wide_copy(values, v_send, v_recv, to, chip).wait_send()
        return carry

    def drain_wide_pass(source, carry):
        wide_pass(keys, kf_send, kf_recv, core, source).wait_send()
        wide_pass(values, vf_send, vf_recv, core, source).wait_send()
        return carry

    lax.fori_loop(1, N, drain, 0)
    lax.fori_loop(1, CHIPS, drain_map, 0)
    lax.fori_loop(0, CHIPS, drain_pass, 0)
    lax.fori_loop(chip + 1, CHIPS, drain_wide, 0)
    lax.fori_loop(0, chip + 1, drain_wide_pass, 0)
    for copy in stores:
        copy.wait()


def place_kernel(count, sums_ref, *refs):
    ins, outs = refs[:count], refs[count : 2 * count]
    log_ref, gain_ref = refs[2 * count : 2 * count + 2]
    held, sems = refs[2 * count + 2 : 3 * count + 2], refs[3 * count + 2]
    first = [pltpu.make_async_copy(a, b, sems.at[0, i]) for i, (a, b) in enumerate(zip(ins, held))]
    second = [pltpu.make_async_copy(a, b, sems.at[1, i]) for i, (a, b) in enumerate(zip(held, outs))]
    for copy in first:
        copy.start()
    log_ref[...] = sums_ref[0:1, 0:HEADS]
    gain_ref[...] = sums_ref[HEADS : HEADS + 1, :]
    for arrives, leaves in zip(first, second):
        arrives.wait()
        leaves.start()
    for copy in second:
        copy.wait()


VM = pl.BlockSpec(memory_space=pltpu.VMEM)
SM = pl.BlockSpec(memory_space=pltpu.SMEM)
ANY = pl.BlockSpec(memory_space=pl.ANY)


def per_device(
    delta_query, delta_key, delta_value, beta_logit, decay_input, decay_log, norm_gain,
    output_gate, delta_cotangent, attn_query, attn_key, attn_value, attn_gate, attn_cotangent,
):
    wide, flat, own = (C, HEADS * DK), (C, GROUP * AD), (C, AD)
    rows, pair = (HEADS, C), (2 * HEADS, DK)
    square, states = (HEADS, DK, DK), (N, SROWS, DK)
    loaded = (N, SROWS + KEEP, DK)
    blocks = (CHIPS, C, 2 * AD)
    args = (
        delta_query[0], delta_key[0], delta_value[0], beta_logit[0].T, decay_input[0].T, decay_log,
        norm_gain[None], output_gate[0], delta_cotangent[0],
        attn_query[0], attn_key[0], attn_value[0], attn_gate[0], attn_cotangent[0],
    )

    def vm(shape, dtype=f32):
        return pltpu.VMEM(shape, dtype)

    def dma(count):
        return pltpu.SemaphoreType.DMA((count,))

    one = pltpu.SemaphoreType.DMA
    shapes = [(wide, bf16)] * 4 + [(rows, f32)] * 2 + [(wide, bf16)]
    shapes += [(flat, bf16)] * 2 + [(own, bf16)] * 2 + [(flat, bf16), (pair, f32)]
    shapes = [jax.ShapeDtypeStruct(s, d) for s, d in shapes]
    results = pl.pallas_call(
        whole_kernel,
        out_shape=tuple(shapes),
        in_specs=[ANY if i in (9, 12, 13) else SM if x.ndim == 1 else VM for i, x in enumerate(args)],
        out_specs=tuple(ANY if i in (0, 1, 2, 3, 6, 7, 8, 11) else VM for i in range(len(shapes))),
        scratch_shapes=[vm(flat, bf16)] * 3
        + [vm(wide, bf16)] * 5
        + [vm(flat, bf16)] * 3
        + [dma(3), dma(8)]
        + [vm((C, HEADS)), vm((C, HEADS)), vm(rows)]
        + [vm(square)] * 6
        + [vm(square, bf16), vm(loaded, bf16), vm((N, DK, DK), bf16), vm(loaded, bf16)]
        + [vm((N, 8, DK))]
        + [vm(states, bf16)] * 6
        + [vm((LENGTH, AD), bf16)] * 2
        + [vm((ROWS, AD), bf16)] * 2
        + [vm((LENGTH, ROWS)), vm((AD, ROWS)), vm((AD, ROWS))]
        + [vm((8, ROWS))] * 3
        + [vm((KB, 2 * AD)), vm(blocks)]
        + [vm(blocks, bf16)] * 4
        + [vm(pair), vm(pair), vm(pair), vm((CHIPS,) + pair), vm(pair), vm((3,) + pair)]
        + [dma(N)] * 12
        + [dma(CHIPS)] * 12
        + [one, one]
        + [dma(CHIPS)] * 2
        + [dma(3)] * 2,
        compiler_params=pltpu.CompilerParams(
            vmem_limit_bytes=VMEM_BIG, collective_id=1, has_side_effects=True
        ),
    )(*args)
    results, sums = results[:-1], results[-1]
    count = len(results)
    *placed, log_grad, gain_grad = pl.pallas_call(
        functools.partial(place_kernel, count),
        out_shape=tuple(shapes[:-1])
        + (jax.ShapeDtypeStruct((1, HEADS), f32), jax.ShapeDtypeStruct((1, DK), f32)),
        in_specs=[VM] + [ANY] * count,
        out_specs=(ANY,) * count + (VM, VM),
        scratch_shapes=[vm(x.shape, x.dtype) for x in results]
        + [pltpu.SemaphoreType.DMA((2, count))],
        compiler_params=pltpu.CompilerParams(vmem_limit_bytes=VMEM_BIG),
    )(sums, *results)
    out, dq, dk, dv, dbl, ddi, dgate, aout, adq, adk, adv, adgate = placed
    return (
        out[None], dq[None], dk[None], dv[None], dbl.T[None], ddi.T[None], log_grad[0], gain_grad[0],
        dgate[None], aout[None], adq[None], adk[None], adv[None], adgate[None],
    )


def solution(mesh):
    split3 = P("section", "ctx", "head")
    in_specs = (split3,) * 5 + (P("head"), P()) + (split3,) * 7
    out_specs = (split3,) * 6 + (P("head"), P()) + (split3,) * 6
    return jax.shard_map(
        per_device, mesh=mesh, in_specs=in_specs, out_specs=out_specs, check_vma=False
    )
```
